512 devices in a mesh: gz: 16 (over y, x_lo), gy: 32 (over x_hi, z, core).
Axes of the slice: x: 4 (x_hi: 2, x_lo: 2; x = x_hi * 2 + x_lo), y: 8, z: 8, core: 2. Of those that a mesh axis runs over, the one named last changes fastest.
Arguments:
- source: bfloat16 [48, 96, 128, 128], P('gz', 'gy'), may hold values from -6 to 6
- target: bfloat16 [48, 96, 128, 128], P('gz', 'gy'), may hold values from -6 to 6
- hidden: bfloat16 [48, 96, 96, 128], P('gz', 'gy'), may hold values from -1 to 1
- motion: float32 [48, 96, 3, 128], P('gz', 'gy'), may hold values from -6 to 6
- w_corr: bfloat16 [96, 343], replicated, may hold values from -0.3125 to 0.3125
- w_motion: float32 [96, 3], replicated, may hold values from -3.5 to 3.5
- bias_encoder: float32 [96], replicated, may hold values from -3 to 3
- w_update: bfloat16 [27, 18432], replicated, may hold values from -0.078125 to 0.078125
- bias_update: float32 [96], replicated, may hold values from -4 to 4
- w_reset: bfloat16 [27, 18432], replicated, may hold values from -0.078125 to 0.078125
- bias_reset: float32 [96], replicated, may hold values from -4 to 4
- w_cand: bfloat16 [27, 18432], replicated, may hold values from -0.078125 to 0.078125
- bias_cand: float32 [96], replicated, may hold values from -3 to 3
- w_head: bfloat16 [27, 3, 96], replicated, may hold values from -0.125 to 0.125
- bias_head: float32 [3], replicated, may hold values from -3 to 3
Outputs:
- state_out: bfloat16 [48, 96, 96, 128], P('gz', 'gy')
- motion_out: float32 [48, 96, 3, 128], P('gz', 'gy')
The draws below stay inside these ranges and needn't reach their ends.
All inputs are finite; a program needn't handle non-finite values.
Results may differ from the reference program's by a relative error of at most 0.0046.
Values may be sent and summed in bfloat16 or wider, within the bound.
A program may use at most 64 MiB of HBM per device.

```python
import jax
import jax.numpy as jnp
from jax import lax

FC = 128
HC = 96
OFFSETS = 343
XW = 128
Z = 48
Y = 96


def block_scale(rng, shape, cuts, smallest, high):
    factor_of, own = 1.0, jax.random.fold_in(rng, 6)
    for axis_at, shards_of in cuts:
        steps = jnp.exp(jax.random.uniform(jax.random.fold_in(own, axis_at), (shards_of,), jnp.float32, smallest / len(cuts), high / len(cuts)))
        factor_of = factor_of * jnp.repeat(steps, shape[axis_at] // shards_of).reshape([-1 if axis == axis_at else 1 for axis in range(len(shape))])
    return factor_of


def normal_values(rng, dims, spread, limit, cuts=(), held_as=jnp.bfloat16):
    array = jax.random.normal(rng, dims, jnp.float32) * spread
    if len(cuts) > 0:
        array = block_scale(rng, dims, cuts, -0.22, 0.18) * array
    return jnp.clip(array, min=-limit, max=limit).astype(held_as)


def setup_inputs(seed: int = 0) -> dict:
    arg_keys = jax.random.split(jax.random.key(seed), 16)
    source = normal_values(arg_keys[0], (Z, Y, FC, XW), 1.0, 6.0, ((0, 16), (1, 32)))
    target = normal_values(arg_keys[1], (Z, Y, FC, XW), 1.0, 6.0, ((0, 16), (1, 32)))
    hidden = jnp.clip(jax.random.uniform(arg_keys[2], (Z, Y, HC, XW), jnp.float32, -1.0, 1.0) * block_scale(arg_keys[2], (Z, Y, HC, XW), ((0, 16), (1, 32)), -0.4, 0.0), -1.0, 1.0).astype(jnp.bfloat16)
    motion = normal_values(arg_keys[3], (Z, Y, 3, XW), 1.0, 6.0, ((0, 16), (1, 32)), jnp.float32)
    w_corr = normal_values(arg_keys[4], (HC, OFFSETS), OFFSETS ** -0.5, 0.3125)
    w_motion = normal_values(arg_keys[5], (HC, 3), 3 ** -0.5, 3.5, (), jnp.float32)
    bias_encoder = normal_values(arg_keys[6], (HC,), 0.5, 3.0, (), jnp.float32)
    w_update = normal_values(arg_keys[7], (27, 2 * HC * HC), (54 * HC) ** -0.5, 0.078125)
    bias_update = normal_values(arg_keys[8], (HC,), 1.0, 4.0, (), jnp.float32)
    w_reset = normal_values(arg_keys[9], (27, 2 * HC * HC), (54 * HC) ** -0.5, 0.078125)
    bias_reset = normal_values(arg_keys[10], (HC,), 1.0, 4.0, (), jnp.float32)
    w_cand = normal_values(arg_keys[11], (27, 2 * HC * HC), (54 * HC) ** -0.5, 0.078125)
    bias_cand = normal_values(arg_keys[12], (HC,), 0.5, 3.0, (), jnp.float32)
    w_head = normal_values(arg_keys[13], (27, 3, HC), (27 * HC) ** -0.5, 0.125)
    bias_head = normal_values(arg_keys[14], (3,), 0.5, 3.0, (), jnp.float32)
    return dict(source=source, target=target, hidden=hidden, motion=motion, w_corr=w_corr, w_motion=w_motion, bias_encoder=bias_encoder, w_update=w_update, bias_update=bias_update, w_reset=w_reset, bias_reset=bias_reset, w_cand=w_cand, bias_cand=bias_cand, w_head=w_head, bias_head=bias_head)


def conv_full(field_in, weight):
    if weight.ndim == 2:
        out_width = field_in.shape[2] // 2
        weight = weight.reshape(27, out_width, field_in.shape[2])
    padded = jnp.pad(field_in.astype(jnp.float32), ((1, 1), (1, 1), (0, 0), (1, 1)))
    depth_cells, row_cells = field_in.shape[0], field_in.shape[1]
    col_cells = field_in.shape[3]
    weight_wide = weight.astype(jnp.float32)
    summed = jnp.zeros((depth_cells, row_cells, weight.shape[1], col_cells), jnp.float32)
    for tap_index in range(27):
        depth_off, row_off, col_off = tap_index // 9, (tap_index // 3) % 3, tap_index % 3
        tap_field = padded[depth_off:depth_off + depth_cells, row_off:row_off + row_cells, :, col_off:col_off + col_cells]
        summed = summed + jnp.einsum('oi,zyix->zyox', weight_wide[tap_index], tap_field)
    return summed


def expand(bias_vector):
    return bias_vector[None, None, :, None]


def reference(source, target, hidden, motion, w_corr, w_motion, bias_encoder, w_update, bias_update, w_reset, bias_reset, w_cand, bias_cand, w_head, bias_head):
    depth_cells, row_cells, channels, col_cells = source.shape
    state_width = hidden.shape[2]
    corr_scale = channels ** -0.5
    source_wide = source.astype(jnp.float32)
    padded_target = jnp.pad(target, ((3, 3), (3, 3), (0, 0), (3, 3)))
    zero_index = jnp.zeros((), jnp.int32)

    def one_pair(summed, offset_pair):
        depth_off = (offset_pair // 7).astype(jnp.int32)
        row_off = (offset_pair % 7).astype(jnp.int32)
        target_slab = lax.dynamic_slice(padded_target, (depth_off, row_off, zero_index, zero_index), (depth_cells, row_cells, channels, col_cells + 6))
        planes = []
        for col_off in range(7):
            shifted = target_slab[..., col_off:col_off + col_cells].astype(jnp.float32)
            planes.append(jnp.sum(source_wide * shifted, axis=2) * corr_scale)
        correlation = jnp.stack(planes, 2).astype(jnp.bfloat16)
        weight_block = lax.dynamic_slice_in_dim(w_corr, (offset_pair * 7).astype(jnp.int32), 7, 1)
        summed = summed + jnp.einsum('ok,zykx->zyox', weight_block.astype(jnp.float32), correlation.astype(jnp.float32))
        return summed, None

    start = jnp.zeros((depth_cells, row_cells, w_corr.shape[0], col_cells), jnp.float32)
    summed, _ = lax.scan(one_pair, start, jnp.arange(49, dtype=jnp.int32))
    summed = summed + jnp.einsum('ok,zykx->zyox', w_motion, motion, precision=lax.Precision.HIGHEST)
    encoded = jax.nn.relu(summed + expand(bias_encoder)).astype(jnp.bfloat16)
    joined = jnp.concatenate([hidden, encoded], 2)
    update_gate = jax.nn.sigmoid(conv_full(joined, w_update) + expand(bias_update))
    reset_gate = jax.nn.sigmoid(conv_full(joined, w_reset) + expand(bias_reset))
    gated_state = (reset_gate * hidden).astype(jnp.bfloat16)
    candidate = jnp.tanh(conv_full(jnp.concatenate([gated_state, encoded], 2), w_cand) + expand(bias_cand))
    state_out = ((1.0 - update_gate) * hidden + update_gate * candidate).astype(jnp.bfloat16)
    motion_out = motion + conv_full(state_out, w_head) + expand(bias_head)
    return state_out, motion_out
```

```python
import functools

import jax
import jax.numpy as jnp
from jax import lax
from jax.experimental import pallas as pl
from jax.experimental.pallas import tpu as pltpu
from jax.sharding import PartitionSpec as P

MESH = pl.DeviceIdType.MESH
F32 = jnp.float32
BF16 = jnp.bfloat16
DIRS = [(dz, dy) for dz in (-1, 0, 1) for dy in (-1, 0, 1) if (dz, dy) != (0, 0)]


def iota(shape, dim):
    return lax.broadcasted_iota(jnp.int32, shape, dim)


def kernel(nz, ny,
           src_hbm, tgt_hbm, hid_hbm, motion, w_corr, w_motion, b_enc, w_upd, b_upd, w_res, b_res, w_cand, b_cand, w_head, b_head,
           state_out, motion_out,
           src, text, hext, eext, gext, sext, wraw, tmp_h, tmp_e, wh, we, wc, whead, headtmp, st, corr, ph, pe,
           loc_sem, blk_send, blk_recv, rim_send, rim_recv):
    gz = lax.axis_index("gz")
    gy = lax.axis_index("gy")
    odd = gz % 2
    s = 1 - 2 * odd
    has_relay_dst = (gz + 2 * s >= 0) & (gz + 2 * s < nz)
    has_relay = (gz - s >= 0) & (gz - s < nz)
    part_plane = 3 + 3 * s
    relay_plane = 3 - 3 * s

    local = []

    def fetch(a, b):
        c = pltpu.make_async_copy(a, b, loc_sem.at[len(local)])
        c.start()
        local.append(c)

    fetch(tgt_hbm, text.at[pl.ds(3, 3), pl.ds(3, 3)])
    fetch(src_hbm, src)
    fetch(hid_hbm, hext.at[pl.ds(1, 3), pl.ds(1, 3)])
    fetch(w_res, wraw.at[0])
    fetch(w_upd, wraw.at[1])
    fetch(w_cand, wraw.at[2])

    barrier = pltpu.get_barrier_semaphore()

    def exists(dz, dy):
        ok = (gz + dz >= 0) & (gz + dz < nz)
        return ok & (gy + dy >= 0) & (gy + dy < ny)

    others = DIRS + [(-2, 0), (2, 0)]
    for dz, dy in others:
        @pl.when(exists(dz, dy))
        def _():
            pl.semaphore_signal(barrier, inc=1, device_id=(gz + dz, gy + dy), device_id_type=MESH)

    for cond, at in (
        (gz == 0, (0, None)), (gz == nz - 1, (1, None)), (gy == 0, (None, 0)), (gy == ny - 1, (None, 1)),
    ):
        @pl.when(cond)
        def _():
            if at[0] is not None:
                def zp(i, c):
                    text[6 * at[0] + i // 9, i % 9] = jnp.zeros((128, 128), BF16)
                    return c
                lax.fori_loop(0, 27, zp, 0)
                for e in (hext, eext, gext, sext):
                    def ze(i, c):
                        e[4 * at[0], i] = jnp.zeros((96, 128), BF16)
                        return c
                    lax.fori_loop(0, 5, ze, 0)
            else:
                def zp(i, c):
                    text[i // 3, 6 * at[1] + i % 3] = jnp.zeros((128, 128), BF16)
                    return c
                lax.fori_loop(0, 27, zp, 0)
                for e in (hext, eext, gext, sext):
                    def ze(i, c):
                        e[i, 4 * at[1]] = jnp.zeros((96, 128), BF16)
                        return c
                    lax.fori_loop(0, 5, ze, 0)

    local[0].wait()
    local[2].wait()
    zs = sum((d + nz - 1) // nz for d in (gz, nz - 1 - gz))
    ys = sum((d + ny - 1) // ny for d in (gy, ny - 1 - gy))
    zs2 = sum((d + nz - 2) // nz for d in (gz, nz - 1 - gz))
    pl.semaphore_wait(barrier, (1 + zs) * (1 + ys) - 1 + zs2)

    def partner_copy(k):
        return pltpu.make_async_remote_copy(
            src_ref=text.at[3 + k, pl.ds(3, 3)], dst_ref=text.at[relay_plane + k, pl.ds(3, 3)],
            send_sem=blk_send.at[k], recv_sem=blk_recv.at[k],
            device_id=(gz + s, gy), device_id_type=MESH)

    def relay_copy(k):
        return pltpu.make_async_remote_copy(
            src_ref=text.at[part_plane + k, pl.ds(3, 3)], dst_ref=text.at[relay_plane + k, pl.ds(3, 3)],
            send_sem=blk_send.at[3 + k], recv_sem=blk_recv.at[3 + k],
            device_id=(gz + 2 * s, gy), device_id_type=MESH)

    def row_copy(group, k, side):
        plane = (3, part_plane, relay_plane)[group] + k
        i = 6 + (group * 3 + k) * 2 + side
        return pltpu.make_async_remote_copy(
            src_ref=text.at[plane, pl.ds(3, 3)], dst_ref=text.at[plane, pl.ds(6 - 6 * side, 3)],
            send_sem=blk_send.at[i], recv_sem=blk_recv.at[i],
            device_id=(gz, gy + 2 * side - 1), device_id_type=MESH)

    side_ok = (gy > 0, gy < ny - 1)

    def rows_start(group, k):
        for side in (0, 1):
            @pl.when(side_ok[side])
            def _():
                row_copy(group, k, side).start()

    def rows_recv(group, k):
        for side in (0, 1):
            @pl.when(side_ok[1 - side])
            def _():
                row_copy(group, k, side).wait_recv()

    def rows_sent(group, k):
        for side in (0, 1):
            @pl.when(side_ok[side])
            def _():
                row_copy(group, k, side).wait_send()

    for k in range(3):
        partner_copy(k).start()
        rows_start(0, k)

    def rim_copy(rnd, ref, d):
        dz, dy = DIRS[d]

        def sl(o, here):
            if o == 0:
                return pl.ds(1, 3)
            return pl.ds((3 if o > 0 else 1) if here else (0 if o > 0 else 4), 1)
        return pltpu.make_async_remote_copy(
            src_ref=ref.at[sl(dz, True), sl(dy, True)], dst_ref=ref.at[sl(dz, False), sl(dy, False)],
            send_sem=rim_send.at[rnd * 8 + d], recv_sem=rim_recv.at[rnd * 8 + d],
            device_id=(gz + dz, gy + dy), device_id_type=MESH)

    def rim_start(rnd, ref):
        for d, (dz, dy) in enumerate(DIRS):
            @pl.when(exists(dz, dy))
            def _():
                rim_copy(rnd, ref, d).start()

    def rim_recv_all(rnd, ref):
        for d, (dz, dy) in enumerate(DIRS):
            @pl.when(exists(-dz, -dy))
            def _():
                rim_copy(rnd, ref, d).wait_recv()

    def rim_sent(rnd, ref):
        for d, (dz, dy) in enumerate(DIRS):
            @pl.when(exists(dz, dy))
            def _():
                rim_copy(rnd, ref, d).wait_send()

    rim_start(0, hext)

    lane8 = iota((8, 128), 1)
    row8 = iota((8, 128), 0)
    flip = jnp.where(iota((128, 128), 0) + iota((128, 128), 1) == 127, 1.0, 0.0).astype(BF16)

    for a in range(7):
        kk = iota((343, 128), 1)
        want = a * 49 + (kk // 8) * 7 + kk % 8
        pick = (iota((343, 128), 0) == want) & (kk % 8 < 7) & (kk < 56)
        wc[:, a * 128:(a + 1) * 128] = jnp.dot(
            w_corr[...], jnp.where(pick, 1.0, 0.0).astype(BF16), preferred_element_type=F32).astype(BF16)

    local[1].wait()

    def turn(p, c):
        st[p] = lax.dot_general(
            flip, src[p // 3, p % 3], (((1,), (1,)), ((), ())), preferred_element_type=F32).astype(BF16)
        return c
    lax.fori_loop(0, 9, turn, 0)

    headtmp[...] = jnp.zeros_like(headtmp)
    for ab in range(9):
        for c in range(3):
            headtmp[c * 8:c * 8 + 3, ab * 96:(ab + 1) * 96] = w_head[ab * 3 + c].astype(F32)
    whead[...] = headtmp[...].astype(BF16)

    for c in local[3:]:
        c.wait()

    def prep(w, carry):
        def spread(op, c):
            x = wraw[w, :, pl.ds(pl.multiple_of(op * 384, 384), 384)].astype(F32)
            r = pl.multiple_of(op * 64, 64)
            tmp_h[pl.ds(r, 27), 0:96] = x[:, 0:96]
            tmp_e[pl.ds(r, 27), 0:96] = x[:, 96:192]
            tmp_h[pl.ds(r + 32, 27), 0:96] = x[:, 192:288]
            tmp_e[pl.ds(r + 32, 27), 0:96] = x[:, 288:384]
            return c
        lax.fori_loop(0, 48, spread, 0)
        for tmp, dst in ((tmp_h, wh), (tmp_e, we)):
            for ab in range(9):
                for c in range(3):
                    v = tmp[pl.ds(ab * 3 + c, 96, stride=32), :]
                    dst[pl.ds(pl.multiple_of(w * 288 + c * 96, 96), 96), ab * 96:(ab + 1) * 96] = v[:, 0:96].astype(BF16)

        @pl.when(w == 0)
        def _():
            for k in range(3):
                partner_copy(k).wait_recv()

                @pl.when(has_relay_dst)
                def _():
                    relay_copy(k).start()
                rows_start(1, k)

        @pl.when((w == 1) & has_relay)
        def _():
            for k in range(3):
                relay_copy(k).wait_recv()
                rows_start(2, k)
        return carry
    lax.fori_loop(0, 3, prep, 0)

    half = lane8 < 64

    def corr_tile(z, y, zt):
        p = z * 3 + y
        lhs = st[p]
        mixed = []
        for b in range(7):
            g = jnp.dot(lhs, text[zt, y + b], preferred_element_type=F32)
            skewed = []
            for par in range(2):
                v = g[8 * par:8 * par + 8]
                for r in range(par + 2, 16, 2):
                    v = jnp.where(lane8 < 132 - 8 * r, g[8 * r:8 * r + 8], v)
                skewed.append(pltpu.roll(v, 4, 1, stride=1, stride_axis=0))
            mixed.append(jnp.where((lane8 & 8) == 0, skewed[0], skewed[1]))
        mixed.append(jnp.zeros((8, 128), F32))
        for d in (1, 2, 4):
            new = list(mixed)
            keep = (lane8 & (8 * d)) == 0
            for i in range(8):
                if not i & d:
                    lo, hi = mixed[i], mixed[i + d]
                    new[i] = jnp.where(keep, lo, pltpu.roll(hi, 8 * d, 1))
                    new[i + d] = jnp.where(keep, pltpu.roll(lo, 128 - 8 * d, 1), hi)
            mixed = new
        rows = []
        for r in range(16):
            group = (16 - r) % 16
            v = mixed[group % 8]
            if group >= 8:
                v = pltpu.roll(v, 64, 1)
            keep = half
            if r in (0, 15):
                xt = 127 - 8 * r - row8 + (lane8 & 7) - 3
                keep = keep & (xt >= 0) & (xt < 128)
            rows.append(jnp.where(keep, v, 0.0))
        tile = (jnp.concatenate(rows, axis=0) * (128.0 ** -0.5)).astype(BF16)
        corr[p * 7 + zt - z] = tile

    for k in range(3):
        rows_recv(0, k)

    def own(i, c):
        corr_tile(i // 9, i // 3 % 3, 3 + i % 3)
        return c
    lax.fori_loop(0, 27, own, 0)

    for k in range(3):
        rows_recv(1, k)

    @pl.when(has_relay)
    def _():
        for k in range(3):
            rows_recv(2, k)

    def outer(up, k, i):
        z, zt = k + i // 3, 6 + k
        corr_tile((1 - up) * (2 - z) + up * z, i % 3, (1 - up) * (8 - zt) + up * zt)

    for k in range(3):
        def both(i, c):
            n = 3 * (3 - k)
            outer(i // n, k, i % n)
            return c
        lax.fori_loop(0, 6 * (3 - k), both, 0)

    back = 127 - iota((8, 128), 1)

    def encode(p, carry):
        z, y = p // 3, p % 3
        acc = jnp.zeros((96, 128), F32)
        for a in range(7):
            acc = acc + lax.dot_general(
                wc[:, a * 128:(a + 1) * 128], corr[p * 7 + a], (((1,), (1,)), ((), ())), preferred_element_type=F32)
        m = motion[z, y]
        term = jnp.zeros((96, 128), F32)
        for j in range(3):
            mj = jnp.broadcast_to(m[j:j + 1], (8, 128))
            mj = jnp.take_along_axis(mj, back, axis=1, mode="promise_in_bounds")
            term = term + w_motion[:, j:j + 1] * jnp.concatenate([mj] * 12, axis=0)
        e = jnp.maximum(acc + term + b_enc[...], 0.0).astype(BF16)
        eext[1 + z, 1 + y] = jnp.dot(e, flip, preferred_element_type=F32).astype(BF16)
        return carry
    lax.fori_loop(0, 9, encode, 0)
    rim_start(1, eext)

    def field(ref):
        cols = []
        for p in range(9):
            z, y = p // 3, p % 3
            cols.append(jnp.concatenate([ref[z + a, y + b] for a in range(3) for b in range(3)], axis=0))
        return jnp.concatenate(cols, axis=1)

    def shifted(parts, p):
        lane = iota((parts[0].shape[0], 128), 1)
        cut = slice(p * 128, (p + 1) * 128)
        left = jnp.where(lane == 0, 0.0, pltpu.roll(parts[0][:, cut], 1, 1))
        right = jnp.where(lane == 127, 0.0, pltpu.roll(parts[2][:, cut], 127, 1))
        return left + parts[1][:, cut] + right

    rim_recv_all(0, hext)
    ph[...] = jnp.dot(wh[0:576], field(hext), preferred_element_type=F32)
    rim_recv_all(1, eext)
    pe[0:288] = jnp.dot(we[0:288], field(eext), preferred_element_type=F32) + ph[0:288]

    def pick(ref, base):
        return [ref[base + c * 96:base + (c + 1) * 96] for c in range(3)]

    for p in range(9):
        z, y = p // 3, p % 3
        r = jax.nn.sigmoid(shifted(pick(pe, 0), p) + b_res[...])
        gext[1 + z, 1 + y] = (r * hext[1 + z, 1 + y].astype(F32)).astype(BF16)
    rim_start(2, gext)

    pe[288:864] = jnp.dot(we[288:864], field(eext), preferred_element_type=F32)
    for c in range(3):
        ph[288 + c * 96:288 + (c + 1) * 96] += pe[288 + c * 96:288 + (c + 1) * 96]
    for p in range(9):
        ph[0:96, p * 128:(p + 1) * 128] = jax.nn.sigmoid(shifted(pick(ph, 288), p) + b_upd[...])
    rim_recv_all(2, gext)
    pe[0:288] = jnp.dot(wh[576:864], field(gext), preferred_element_type=F32) + pe[576:864]
    for p in range(9):
        z, y = p // 3, p % 3
        cand = jnp.tanh(shifted(pick(pe, 0), p) + b_cand[...])
        u = ph[0:96, p * 128:(p + 1) * 128]
        new = ((1.0 - u) * hext[1 + z, 1 + y].astype(F32) + u * cand).astype(BF16)
        sext[1 + z, 1 + y] = new
        state_out[z, y] = new
    rim_start(3, sext)
    rim_recv_all(3, sext)
    pe[0:24] = jnp.dot(whead[...], field(sext), preferred_element_type=F32)
    for p in range(9):
        z, y = p // 3, p % 3
        out = shifted([pe[c * 8:(c + 1) * 8] for c in range(3)], p)
        motion_out[z, y] = motion[z, y] + out[0:3] + b_head[...]

    for k in range(3):
        partner_copy(k).wait_send()

        @pl.when(has_relay_dst)
        def _():
            relay_copy(k).wait_send()
        rows_sent(0, k)
        rows_sent(1, k)

        @pl.when(has_relay)
        def _():
            rows_sent(2, k)
    for rnd, ref in enumerate((hext, eext, gext, sext)):
        rim_sent(rnd, ref)


def solution(mesh):
    nz, ny = mesh.shape["gz"], mesh.shape["gy"]

    def on_device(source, target, hidden, motion, w_corr, w_motion, bias_encoder, w_update, bias_update, w_reset, bias_reset,
                  w_cand, bias_cand, w_head, bias_head):
        hbm = pl.BlockSpec(memory_space=pl.ANY)
        vmem = pl.BlockSpec(memory_space=pltpu.VMEM)
        ext = pltpu.VMEM((5, 5, 96, 128), BF16)
        return pl.pallas_call(
            functools.partial(kernel, nz, ny),
            name="dvc_update",
            out_shape=(jax.ShapeDtypeStruct((3, 3, 96, 128), BF16), jax.ShapeDtypeStruct((3, 3, 3, 128), F32)),
            in_specs=[hbm, hbm, hbm, vmem, vmem, vmem, vmem, hbm, vmem, hbm, vmem, hbm, vmem, vmem, vmem],
            out_specs=(vmem, vmem),
            scratch_shapes=[
                pltpu.VMEM((3, 3, 128, 128), BF16),
                pltpu.VMEM((9, 9, 128, 128), BF16),
                ext, ext, ext, ext,
                pltpu.VMEM((3, 27, 18432), BF16),
                pltpu.VMEM((3072, 128), F32), pltpu.VMEM((3072, 128), F32),
                pltpu.VMEM((864, 864), BF16), pltpu.VMEM((864, 864), BF16),
                pltpu.VMEM((96, 896), BF16),
                pltpu.VMEM((24, 864), BF16), pltpu.VMEM((24, 864), F32),
                pltpu.VMEM((9, 128, 128), BF16),
                pltpu.VMEM((63, 128, 128), BF16),
                pltpu.VMEM((576, 1152), F32),
                pltpu.VMEM((864, 1152), F32),
                pltpu.SemaphoreType.DMA((6,)),
                pltpu.SemaphoreType.DMA((24,)), pltpu.SemaphoreType.DMA((24,)),
                pltpu.SemaphoreType.DMA((32,)), pltpu.SemaphoreType.DMA((32,)),
            ],
            compiler_params=pltpu.CompilerParams(
                collective_id=0, has_side_effects=True, vmem_limit_bytes=60 * 2 ** 20),
        )(source, target, hidden, motion, w_corr, w_motion, bias_encoder[:, None], w_update, bias_update[:, None], w_reset,
          bias_reset[:, None], w_cand, bias_cand[:, None], w_head, bias_head[:, None])

    rows = P("gz", "gy", None, None)
    return jax.shard_map(
        on_device, mesh=mesh, in_specs=(rows,) * 4 + (P(),) * 11, out_specs=(rows, rows), check_vma=False)
```

```python
import functools

import jax
import jax.numpy as jnp
from jax import lax
from jax.experimental import pallas as pl
from jax.experimental.pallas import tpu as pltpu
from jax.sharding import PartitionSpec as P

MESH = pl.DeviceIdType.MESH
F32 = jnp.float32
BF16 = jnp.bfloat16
GROUPS = ((0, 1), (2, 3), (4, 5), (6, 7), (8,))
DIRS = [(dz, dy) for dz in (-1, 0, 1) for dy in (-1, 0, 1) if (dz, dy) != (0, 0)]


def iota(shape, dim):
    return lax.broadcasted_iota(jnp.int32, shape, dim)


def kernel(nz, ny,
           src_hbm, tgt_hbm, hid_hbm, motion, w_corr, w_motion, b_enc, w_upd, b_upd, w_res, b_res, w_cand, b_cand, w_head, b_head,
           state_out, motion_out,
           src, text, hext, eext, gext, sext, wraw, tmp_h, tmp_e, wh, we, wc, whead, headtmp, st, corr, ph, pe,
           loc_sem, blk_send, blk_recv, rim_send, rim_recv):
    gz = lax.axis_index("gz")
    gy = lax.axis_index("gy")
    odd = gz % 2
    s = 1 - 2 * odd
    has_relay_dst = (gz + 2 * s >= 0) & (gz + 2 * s < nz)
    has_relay = (gz - s >= 0) & (gz - s < nz)
    part_plane = 3 + 3 * s
    relay_plane = 3 - 3 * s

    local = []

    def fetch(a, b):
        c = pltpu.make_async_copy(a, b, loc_sem.at[len(local)])
        c.start()
        local.append(c)

    fetch(tgt_hbm, text.at[pl.ds(3, 3), pl.ds(3, 3)])
    fetch(src_hbm, src)
    fetch(hid_hbm, hext.at[pl.ds(1, 3), pl.ds(1, 3)])
    fetch(w_res, wraw.at[0])
    fetch(w_upd, wraw.at[1])
    fetch(w_cand, wraw.at[2])

    barrier = pltpu.get_barrier_semaphore()

    def exists(dz, dy):
        ok = (gz + dz >= 0) & (gz + dz < nz)
        return ok & (gy + dy >= 0) & (gy + dy < ny)

    others = DIRS + [(-2, 0), (2, 0)]
    for dz, dy in others:
        @pl.when(exists(dz, dy))
        def _():
            pl.semaphore_signal(barrier, inc=1, device_id=(gz + dz, gy + dy), device_id_type=MESH)

    for cond, at in (
        (gz == 0, (0, None)), (gz == nz - 1, (1, None)), (gy == 0, (None, 0)), (gy == ny - 1, (None, 1)),
    ):
        @pl.when(cond)
        def _():
            if at[0] is not None:
                def zp(i, c):
                    text[6 * at[0] + i // 9, i % 9] = jnp.zeros((128, 128), BF16)
                    return c
                lax.fori_loop(0, 27, zp, 0)
                for e in (hext, eext, gext, sext):
                    def ze(i, c):
                        e[4 * at[0], i] = jnp.zeros((96, 128), BF16)
                        return c
                    lax.fori_loop(0, 5, ze, 0)
            else:
                def zp(i, c):
                    text[i // 3, 6 * at[1] + i % 3] = jnp.zeros((128, 128), BF16)
                    return c
                lax.fori_loop(0, 27, zp, 0)
                for e in (hext, eext, gext, sext):
                    def ze(i, c):
                        e[i, 4 * at[1]] = jnp.zeros((96, 128), BF16)
                        return c
                    lax.fori_loop(0, 5, ze, 0)

    local[0].wait()
    local[2].wait()
    zs = sum((d + nz - 1) // nz for d in (gz, nz - 1 - gz))
    ys = sum((d + ny - 1) // ny for d in (gy, ny - 1 - gy))
    zs2 = sum((d + nz - 2) // nz for d in (gz, nz - 1 - gz))
    pl.semaphore_wait(barrier, (1 + zs) * (1 + ys) - 1 + zs2)

    def partner_copy(k):
        return pltpu.make_async_remote_copy(
            src_ref=text.at[3 + k, pl.ds(3, 3)], dst_ref=text.at[relay_plane + k, pl.ds(3, 3)],
            send_sem=blk_send.at[k], recv_sem=blk_recv.at[k],
            device_id=(gz + s, gy), device_id_type=MESH)

    def relay_copy(k):
        return pltpu.make_async_remote_copy(
            src_ref=text.at[part_plane + k, pl.ds(3, 3)], dst_ref=text.at[relay_plane + k, pl.ds(3, 3)],
            send_sem=blk_send.at[3 + k], recv_sem=blk_recv.at[3 + k],
            device_id=(gz + 2 * s, gy), device_id_type=MESH)

    def row_copy(group, k, side):
        plane = (3, part_plane, relay_plane)[group] + k
        i = 6 + (group * 3 + k) * 2 + side
        return pltpu.make_async_remote_copy(
            src_ref=text.at[plane, pl.ds(3, 3)], dst_ref=text.at[plane, pl.ds(6 - 6 * side, 3)],
            send_sem=blk_send.at[i], recv_sem=blk_recv.at[i],
            device_id=(gz, gy + 2 * side - 1), device_id_type=MESH)

    side_ok = (gy > 0, gy < ny - 1)

    def rows_start(group, k):
        for side in (0, 1):
            @pl.when(side_ok[side])
            def _():
                row_copy(group, k, side).start()

    def rows_recv(group, k):
        for side in (0, 1):
            @pl.when(side_ok[1 - side])
            def _():
                row_copy(group, k, side).wait_recv()

    def rows_sent(group, k):
        for side in (0, 1):
            @pl.when(side_ok[side])
            def _():
                row_copy(group, k, side).wait_send()

    for k in range(3):
        partner_copy(k).start()
        rows_start(0, k)

    def rim_copy(rnd, ref, d):
        dz, dy = DIRS[d]

        def sl(o, here):
            if o == 0:
                return pl.ds(1, 3)
            return pl.ds((3 if o > 0 else 1) if here else (0 if o > 0 else 4), 1)
        return pltpu.make_async_remote_copy(
            src_ref=ref.at[sl(dz, True), sl(dy, True)], dst_ref=ref.at[sl(dz, False), sl(dy, False)],
            send_sem=rim_send.at[rnd * 8 + d], recv_sem=rim_recv.at[rnd * 8 + d],
            device_id=(gz + dz, gy + dy), device_id_type=MESH)

    def rim_start(rnd, ref):
        for d, (dz, dy) in enumerate(DIRS):
            @pl.when(exists(dz, dy))
            def _():
                rim_copy(rnd, ref, d).start()

    def rim_recv_all(rnd, ref):
        for d, (dz, dy) in enumerate(DIRS):
            @pl.when(exists(-dz, -dy))
            def _():
                rim_copy(rnd, ref, d).wait_recv()

    def rim_sent(rnd, ref):
        for d, (dz, dy) in enumerate(DIRS):
            @pl.when(exists(dz, dy))
            def _():
                rim_copy(rnd, ref, d).wait_send()

    lane8 = iota((8, 128), 1)
    row8 = iota((8, 128), 0)
    flip = jnp.where(iota((128, 128), 0) + iota((128, 128), 1) == 127, 1.0, 0.0).astype(BF16)

    for a in range(7):
        kk = iota((343, 128), 1)
        want = a * 49 + (kk // 8) * 7 + kk % 8
        pick = (iota((343, 128), 0) == want) & (kk % 8 < 7) & (kk < 56)
        wc[:, a * 128:(a + 1) * 128] = jnp.dot(
            w_corr[...], jnp.where(pick, 1.0, 0.0).astype(BF16), preferred_element_type=F32).astype(BF16)

    local[1].wait()

    for p in range(9):
        st[p * 128:(p + 1) * 128] = lax.dot_general(
            flip, src[p // 3, p % 3], (((1,), (1,)), ((), ())), preferred_element_type=F32).astype(BF16)

    headtmp[...] = jnp.zeros_like(headtmp)
    for o in range(3):
        v = w_head[o].astype(F32)
        for ab in range(9):
            for c in range(3):
                headtmp[c * 8 + o:c * 8 + o + 1, ab * 96:(ab + 1) * 96] = v[ab * 3 + c:ab * 3 + c + 1]
    whead[...] = headtmp[...].astype(BF16)

    def spread(w):
        local[3 + w].wait()

        def some(op4, c):
            for u in range(4):
                op = op4 * 4 + u
                x = wraw[w, :, pl.ds(pl.multiple_of(op * 384, 384), 384)].astype(F32)
                r = pl.multiple_of(op * 64, 64)
                tmp_h[pl.ds(r, 27), 0:96] = x[:, 0:96]
                tmp_e[pl.ds(r, 27), 0:96] = x[:, 96:192]
                tmp_h[pl.ds(r + 32, 27), 0:96] = x[:, 192:288]
                tmp_e[pl.ds(r + 32, 27), 0:96] = x[:, 288:384]
            return c
        lax.fori_loop(0, 12, some, 0)

    def collect(w):
        for tmp, dst in ((tmp_h, wh), (tmp_e, we)):
            for ab in range(9):
                for c in range(3):
                    v = tmp[pl.ds(ab * 3 + c, 96, stride=32), :]
                    row = w * 288 + c * 96
                    dst[row:row + 96, ab * 96:(ab + 1) * 96] = v[:, 0:96].astype(BF16)

    def pass_partner(k):
        partner_copy(k).wait_recv()

        @pl.when(has_relay_dst)
        def _():
            relay_copy(k).start()
        rows_start(1, k)

    def pass_relay(k):
        @pl.when(has_relay)
        def _():
            relay_copy(k).wait_recv()
            rows_start(2, k)

    pass_partner(0)
    spread(0)
    pass_partner(1)
    collect(0)
    pass_partner(2)

    half = lane8 < 64

    def corr_rows(z, zt):
        mixed = [[None] * 8 for _ in range(3)]

        def diagonals(g):
            skewed = []
            for par in range(2):
                v = g(par)
                for r in range(par + 2, 16, 2):
                    v = jnp.where(lane8 < 132 - 8 * r, g(r), v)
                skewed.append(pltpu.roll(v, 4, 1, stride=1, stride_axis=0))
            return jnp.where((lane8 & 8) == 0, skewed[0], skewed[1])

        for group in GROUPS:
            lo = max(0, min(group) - 6)
            hi = min(2, max(group))
            lhs = st[pl.ds(pl.multiple_of((z * 3 + lo) * 128, 128), (hi - lo + 1) * 128)]
            rhs = jnp.concatenate([text[zt, row] for row in group], axis=1)
            g = jnp.dot(lhs, rhs, preferred_element_type=F32)
            for n, row in enumerate(group):
                for y in range(lo, hi + 1):
                    if 0 <= row - y <= 6:
                        mixed[y][row - y] = diagonals(
                            lambda r: g[(y - lo) * 128 + 8 * r:(y - lo) * 128 + 8 * r + 8, n * 128:(n + 1) * 128])
        for y in range(3):
            mix = mixed[y]
            mix[7] = jnp.zeros((8, 128), F32)
            for d in (1, 2, 4):
                new = list(mix)
                keep = (lane8 & (8 * d)) == 0
                for i in range(8):
                    if not i & d:
                        a, b = mix[i], mix[i + d]
                        new[i] = jnp.where(keep, a, pltpu.roll(b, 8 * d, 1))
                        new[i + d] = jnp.where(keep, pltpu.roll(a, 128 - 8 * d, 1), b)
                mix = new
            rows = []
            for r in range(16):
                at = (16 - r) % 16
                v = mix[at % 8]
                if at >= 8:
                    v = pltpu.roll(v, 64, 1)
                keep = half
                if r in (0, 15):
                    xt = 127 - 8 * r - row8 + (lane8 & 7) - 3
                    keep = keep & (xt >= 0) & (xt < 128)
                rows.append(jnp.where(keep, v, 0.0))
            tile = (jnp.concatenate(rows, axis=0) * (128.0 ** -0.5)).astype(BF16)
            corr[pl.ds(pl.multiple_of((z * 3 + y) * 128, 128), 128), pl.ds(pl.multiple_of((zt - z) * 128, 128), 128)] = tile

    for k in range(3):
        rows_recv(0, k)

    def own(i, c):
        corr_rows(i // 3, 3 + i % 3)
        for at, k in ((0, 0), (1, 1), (3, 2)):
            @pl.when(i == at)
            def _():
                pass_relay(k)
        return c
    lax.fori_loop(0, 9, own, 0)
    rim_start(0, hext)

    def side(n, carry):
        up = (1 - odd) * (1 - n) + odd * n

        @pl.when(n == 0)
        def _():
            for k in range(3):
                rows_recv(1, k)

        @pl.when((n == 1) & has_relay)
        def _():
            for k in range(3):
                rows_recv(2, k)
        for k in range(3):
            def cell(z, c):
                zt = 6 + k
                corr_rows((1 - up) * (2 - z) + up * z, (1 - up) * (8 - zt) + up * zt)
                return c
            lax.fori_loop(k, 3, cell, 0)
        return carry
    lax.fori_loop(0, 2, side, 0)

    eye = iota((96, 96), 0) == iota((96, 96), 1)

    def column(row):
        return jnp.sum(jnp.where(eye, jnp.broadcast_to(row, (96, 96)), 0.0), axis=1, keepdims=True)

    pe[0:96] = lax.dot_general(wc[...], corr[...], (((1,), (1,)), ((), ())), preferred_element_type=F32)
    back = 127 - lane8
    enc_bias = jnp.broadcast_to(column(b_enc[...]), (96, 128))
    enc_motion = [jnp.broadcast_to(column(w_motion[j:j + 1]), (96, 128)) for j in range(3)]
    turned = []
    for p in range(9):
        m = motion[p // 3, p % 3]
        e = pe[0:96, p * 128:(p + 1) * 128] + enc_bias
        for j in range(3):
            mj = jnp.take_along_axis(jnp.broadcast_to(m[j:j + 1], (8, 128)), back, axis=1, mode="promise_in_bounds")
            e = e + enc_motion[j] * jnp.concatenate([mj] * 12, axis=0)
        turned.append(jnp.maximum(e, 0.0).astype(BF16))
    straight = jnp.dot(jnp.concatenate(turned, axis=0), flip, preferred_element_type=F32).astype(BF16)
    for p in range(9):
        eext[1 + p // 3, 1 + p % 3] = straight[p * 96:(p + 1) * 96]
    rim_start(1, eext)

    def field(ref):
        cols = []
        for p in range(9):
            z, y = p // 3, p % 3
            cols.append(jnp.concatenate([ref[z + a, y + b] for a in range(3) for b in range(3)], axis=0))
        return jnp.concatenate(cols, axis=1)

    def shifted(parts, p):
        lane = iota((parts[0].shape[0], 128), 1)
        cut = slice(p * 128, (p + 1) * 128)
        left = jnp.where(lane == 0, 0.0, pltpu.roll(parts[0][:, cut], 1, 1))
        right = jnp.where(lane == 127, 0.0, pltpu.roll(parts[2][:, cut], 127, 1))
        return left + parts[1][:, cut] + right

    spread(1)
    collect(1)
    rim_recv_all(0, hext)
    ph[...] = jnp.dot(wh[0:576], field(hext), preferred_element_type=F32)
    rim_recv_all(1, eext)
    pe[0:288] = jnp.dot(we[0:288], field(eext), preferred_element_type=F32) + ph[0:288]

    def pick(ref, base):
        return [ref[base + c * 96:base + (c + 1) * 96] for c in range(3)]

    res_bias = column(b_res[...])
    for p in range(9):
        z, y = p // 3, p % 3
        r = jax.nn.sigmoid(shifted(pick(pe, 0), p) + res_bias)
        gext[1 + z, 1 + y] = (r * hext[1 + z, 1 + y].astype(F32)).astype(BF16)
    rim_start(2, gext)
    spread(2)
    collect(2)

    pe[288:864] = jnp.dot(we[288:864], field(eext), preferred_element_type=F32)
    for c in range(3):
        ph[288 + c * 96:288 + (c + 1) * 96] += pe[288 + c * 96:288 + (c + 1) * 96]
    upd_bias = column(b_upd[...])
    cand_bias = column(b_cand[...])
    for p in range(9):
        ph[0:96, p * 128:(p + 1) * 128] = jax.nn.sigmoid(shifted(pick(ph, 288), p) + upd_bias)
    rim_recv_all(2, gext)
    pe[0:288] = jnp.dot(wh[576:864], field(gext), preferred_element_type=F32) + pe[576:864]
    for p in range(9):
        z, y = p // 3, p % 3
        cand = jnp.tanh(shifted(pick(pe, 0), p) + cand_bias)
        u = ph[0:96, p * 128:(p + 1) * 128]
        new = ((1.0 - u) * hext[1 + z, 1 + y].astype(F32) + u * cand).astype(BF16)
        sext[1 + z, 1 + y] = new
        state_out[z, y] = new
    rim_start(3, sext)
    rim_recv_all(3, sext)
    pe[0:24] = jnp.dot(whead[...], field(sext), preferred_element_type=F32)
    for p in range(9):
        z, y = p // 3, p % 3
        out = shifted([pe[c * 8:(c + 1) * 8] for c in range(3)], p)
        for o in range(3):
            motion_out[z, y, o:o + 1] = motion[z, y, o:o + 1] + out[o:o + 1] + b_head[0:1, o:o + 1]

    for k in range(3):
        partner_copy(k).wait_send()

        @pl.when(has_relay_dst)
        def _():
            relay_copy(k).wait_send()
        rows_sent(0, k)
        rows_sent(1, k)

        @pl.when(has_relay)
        def _():
            rows_sent(2, k)
    for rnd, ref in enumerate((hext, eext, gext, sext)):
        rim_sent(rnd, ref)


def solution(mesh):
    nz, ny = mesh.shape["gz"], mesh.shape["gy"]

    def on_device(source, target, hidden, motion, w_corr, w_motion, bias_encoder, w_update, bias_update, w_reset, bias_reset,
                  w_cand, bias_cand, w_head, bias_head):
        hbm = pl.BlockSpec(memory_space=pl.ANY)
        vmem = pl.BlockSpec(memory_space=pltpu.VMEM)
        ext = pltpu.VMEM((5, 5, 96, 128), BF16)
        return pl.pallas_call(
            functools.partial(kernel, nz, ny),
            name="dvc_update",
            out_shape=(jax.ShapeDtypeStruct((3, 3, 96, 128), BF16), jax.ShapeDtypeStruct((3, 3, 3, 128), F32)),
            in_specs=[hbm, hbm, hbm, vmem, vmem, vmem, vmem, hbm, vmem, hbm, vmem, hbm, vmem, vmem, vmem],
            out_specs=(vmem, vmem),
            scratch_shapes=[
                pltpu.VMEM((3, 3, 128, 128), BF16),
                pltpu.VMEM((9, 9, 128, 128), BF16),
                ext, ext, ext, ext,
                pltpu.VMEM((3, 27, 18432), BF16),
                pltpu.VMEM((3072, 128), F32), pltpu.VMEM((3072, 128), F32),
                pltpu.VMEM((864, 864), BF16), pltpu.VMEM((864, 864), BF16),
                pltpu.VMEM((96, 896), BF16),
                pltpu.VMEM((24, 864), BF16), pltpu.VMEM((24, 864), F32),
                pltpu.VMEM((1152, 128), BF16),
                pltpu.VMEM((1152, 896), BF16),
                pltpu.VMEM((576, 1152), F32),
                pltpu.VMEM((864, 1152), F32),
                pltpu.SemaphoreType.DMA((6,)),
                pltpu.SemaphoreType.DMA((24,)), pltpu.SemaphoreType.DMA((24,)),
                pltpu.SemaphoreType.DMA((32,)), pltpu.SemaphoreType.DMA((32,)),
            ],
            compiler_params=pltpu.CompilerParams(
                collective_id=0, has_side_effects=True, vmem_limit_bytes=60 * 2 ** 20),
        )(source, target, hidden, motion, w_corr, w_motion.T, bias_encoder[None], w_update, bias_update[None], w_reset,
          bias_reset[None], w_cand, bias_cand[None], w_head.transpose(1, 0, 2), bias_head[None])

    rows = P("gz", "gy", None, None)
    return jax.shard_map(
        on_device, mesh=mesh, in_specs=(rows,) * 4 + (P(),) * 11, out_specs=(rows, rows), check_vma=False)
```

```python
import functools

import jax
import jax.numpy as jnp
from jax import lax
from jax.experimental import pallas as pl
from jax.experimental.pallas import tpu as pltpu
from jax.sharding import PartitionSpec as P

MESH = pl.DeviceIdType.MESH
F32 = jnp.float32
BF16 = jnp.bfloat16
GROUPS = tuple((r,) for r in range(9))
DIRS = [(dz, dy) for dz in (-1, 0, 1) for dy in (-1, 0, 1) if (dz, dy) != (0, 0)]


def iota(shape, dim):
    return lax.broadcasted_iota(jnp.int32, shape, dim)


def kernel(nz, ny,
           src_hbm, tgt_hbm, hid_hbm, motion, w_corr, w_motion, b_enc, w_upd, b_upd, w_res, b_res, w_cand, b_cand, w_head, b_head,
           state_out, motion_out,
           src, text, hext, eext, gext, sext, hsend, hrecv, wraw, tmp_h, tmp_e, wh, we, wc, whead, headtmp, st, corr, ph, pe,
           loc_sem, blk_send, blk_recv, rim_send, rim_recv):
    gz = lax.axis_index("gz")
    gy = lax.axis_index("gy")
    odd = gz % 2
    s = 1 - 2 * odd
    has_relay_dst = (gz + 2 * s >= 0) & (gz + 2 * s < nz)
    has_relay = (gz - s >= 0) & (gz - s < nz)
    part_plane = 3 + 3 * s
    relay_plane = 3 - 3 * s

    local = []

    def fetch(a, b):
        c = pltpu.make_async_copy(a, b, loc_sem.at[len(local)])
        c.start()
        local.append(c)

    fetch(tgt_hbm, text.at[pl.ds(3, 3), pl.ds(3, 3)])
    fetch(src_hbm, src)
    fetch(hid_hbm, hext.at[pl.ds(1, 3), pl.ds(1, 3)])
    fetch(w_res, wraw.at[0])
    fetch(w_upd, wraw.at[1])
    fetch(w_cand, wraw.at[2])

    barrier = pltpu.get_barrier_semaphore()

    def exists(dz, dy):
        ok = (gz + dz >= 0) & (gz + dz < nz)
        return ok & (gy + dy >= 0) & (gy + dy < ny)

    others = DIRS + [(-2, 0), (2, 0)]
    for dz, dy in others:
        @pl.when(exists(dz, dy))
        def _():
            pl.semaphore_signal(barrier, inc=1, device_id=(gz + dz, gy + dy), device_id_type=MESH)

    for d, (dz, dy) in enumerate(DIRS):
        @pl.when(jnp.logical_not(exists(-dz, -dy)))
        def _():
            hrecv[d] = jnp.zeros((3, 3, 8, 128), F32)
    for cond, at in (
        (gz == 0, (0, None)), (gz == nz - 1, (1, None)), (gy == 0, (None, 0)), (gy == ny - 1, (None, 1)),
    ):
        @pl.when(cond)
        def _():
            if at[0] is not None:
                def zp(i, c):
                    text[6 * at[0] + i // 9, i % 9] = jnp.zeros((128, 128), BF16)
                    return c
                lax.fori_loop(0, 27, zp, 0)
                for e in (hext, eext, gext):
                    def ze(i, c):
                        e[4 * at[0], i] = jnp.zeros((96, 128), BF16)
                        return c
                    lax.fori_loop(0, 5, ze, 0)
            else:
                def zp(i, c):
                    text[i // 3, 6 * at[1] + i % 3] = jnp.zeros((128, 128), BF16)
                    return c
                lax.fori_loop(0, 27, zp, 0)
                for e in (hext, eext, gext):
                    def ze(i, c):
                        e[i, 4 * at[1]] = jnp.zeros((96, 128), BF16)
                        return c
                    lax.fori_loop(0, 5, ze, 0)

    lane8 = iota((8, 128), 1)
    row8 = iota((8, 128), 0)
    flip = jnp.where(iota((128, 128), 0) + iota((128, 128), 1) == 127, 1.0, 0.0).astype(BF16)

    for a in range(7):
        kk = iota((343, 128), 1)
        want = a * 49 + (kk // 8) * 7 + kk % 8
        pick = (iota((343, 128), 0) == want) & (kk % 8 < 7) & (kk < 56)
        wc[:, a * 128:(a + 1) * 128] = jnp.dot(
            w_corr[...], jnp.where(pick, 1.0, 0.0).astype(BF16), preferred_element_type=F32).astype(BF16)

    local[1].wait()

    for p in range(9):
        st[p * 128:(p + 1) * 128] = lax.dot_general(
            flip, src[p // 3, p % 3], (((1,), (1,)), ((), ())), preferred_element_type=F32).astype(BF16)

    headtmp[...] = jnp.zeros_like(headtmp)
    for o in range(3):
        headtmp[pl.ds(o, 27, stride=8), :] = jnp.concatenate([w_head[o].astype(F32), jnp.zeros((27, 32), F32)], axis=1)
    whead[...] = headtmp[...].astype(BF16)

    local[0].wait()
    local[2].wait()
    zs = sum((d + nz - 1) // nz for d in (gz, nz - 1 - gz))
    ys = sum((d + ny - 1) // ny for d in (gy, ny - 1 - gy))
    zs2 = sum((d + nz - 2) // nz for d in (gz, nz - 1 - gz))
    pl.semaphore_wait(barrier, (1 + zs) * (1 + ys) - 1 + zs2)

    def partner_copy(k):
        return pltpu.make_async_remote_copy(
            src_ref=text.at[3 + k, pl.ds(3, 3)], dst_ref=text.at[relay_plane + k, pl.ds(3, 3)],
            send_sem=blk_send.at[k], recv_sem=blk_recv.at[k],
            device_id=(gz + s, gy), device_id_type=MESH)

    def relay_copy(k):
        return pltpu.make_async_remote_copy(
            src_ref=text.at[part_plane + k, pl.ds(3, 3)], dst_ref=text.at[relay_plane + k, pl.ds(3, 3)],
            send_sem=blk_send.at[3 + k], recv_sem=blk_recv.at[3 + k],
            device_id=(gz + 2 * s, gy), device_id_type=MESH)

    def row_copy(group, k, side):
        plane = (3, part_plane, relay_plane)[group] + k
        i = 6 + (group * 3 + k) * 2 + side
        return pltpu.make_async_remote_copy(
            src_ref=text.at[plane, pl.ds(3, 3)], dst_ref=text.at[plane, pl.ds(6 - 6 * side, 3)],
            send_sem=blk_send.at[i], recv_sem=blk_recv.at[i],
            device_id=(gz, gy + 2 * side - 1), device_id_type=MESH)

    side_ok = (gy > 0, gy < ny - 1)

    def rows_start(group, k):
        for side in (0, 1):
            @pl.when(side_ok[side])
            def _():
                row_copy(group, k, side).start()

    def rows_recv(group, k):
        for side in (0, 1):
            @pl.when(side_ok[1 - side])
            def _():
                row_copy(group, k, side).wait_recv()

    def rows_sent(group, k):
        for side in (0, 1):
            @pl.when(side_ok[side])
            def _():
                row_copy(group, k, side).wait_send()

    for k in range(3):
        partner_copy(k).start()
        rows_start(0, k)

    def rim_copy(rnd, ref, d):
        dz, dy = DIRS[d]

        def sl(o, here):
            if o == 0:
                return pl.ds(1, 3)
            return pl.ds((3 if o > 0 else 1) if here else (0 if o > 0 else 4), 1)
        return pltpu.make_async_remote_copy(
            src_ref=ref.at[sl(dz, True), sl(dy, True)], dst_ref=ref.at[sl(dz, False), sl(dy, False)],
            send_sem=rim_send.at[rnd * 9 + d], recv_sem=rim_recv.at[rnd * 9 + d],
            device_id=(gz + dz, gy + dy), device_id_type=MESH)

    def rim_start(rnd, ref):
        for d, (dz, dy) in enumerate(DIRS):
            @pl.when(exists(dz, dy))
            def _():
                rim_copy(rnd, ref, d).start()

    def rim_recv_all(rnd, ref):
        for d, (dz, dy) in enumerate(DIRS):
            @pl.when(exists(-dz, -dy))
            def _():
                rim_copy(rnd, ref, d).wait_recv()

    def rim_sent(rnd, ref):
        for d, (dz, dy) in enumerate(DIRS):
            @pl.when(exists(dz, dy))
            def _():
                rim_copy(rnd, ref, d).wait_send()

    def spread(w):
        local[3 + w].wait()

        def some(op4, c):
            for u in range(4):
                op = op4 * 4 + u
                x = wraw[w, :, pl.ds(pl.multiple_of(op * 384, 384), 384)].astype(F32)
                r = pl.multiple_of(op * 64, 64)
                tmp_h[pl.ds(r, 27), 0:96] = x[:, 0:96]
                tmp_e[pl.ds(r, 27), 0:96] = x[:, 96:192]
                tmp_h[pl.ds(r + 32, 27), 0:96] = x[:, 192:288]
                tmp_e[pl.ds(r + 32, 27), 0:96] = x[:, 288:384]
            return c
        lax.fori_loop(0, 12, some, 0)

    def collect(w):
        for tmp, dst in ((tmp_h, wh), (tmp_e, we)):
            for ab in range(9):
                for c in range(3):
                    v = tmp[pl.ds(ab * 3 + c, 96, stride=32), :]
                    row = w * 288 + c * 96
                    dst[row:row + 96, ab * 96:(ab + 1) * 96] = v[:, 0:96].astype(BF16)

    def pass_partner(k):
        partner_copy(k).wait_recv()

        @pl.when(has_relay_dst)
        def _():
            relay_copy(k).start()
        rows_start(1, k)

    def pass_relay(k):
        @pl.when(has_relay)
        def _():
            relay_copy(k).wait_recv()
            rows_start(2, k)

    pass_partner(0)
    spread(0)
    pass_partner(1)
    collect(0)
    pass_partner(2)

    half = lane8 < 64

    def corr_rows(z, zt):
        mixed = [[None] * 8 for _ in range(3)]

        def diagonals(g):
            skewed = []
            for par in range(2):
                v = g(par)
                for r in range(par + 2, 16, 2):
                    v = jnp.where(lane8 < 132 - 8 * r, g(r), v)
                skewed.append(pltpu.roll(v, 4, 1, stride=1, stride_axis=0))
            return jnp.where((lane8 & 8) == 0, skewed[0], skewed[1])

        for group in GROUPS:
            lo = max(0, min(group) - 6)
            hi = min(2, max(group))
            lhs = st[pl.ds(pl.multiple_of((z * 3 + lo) * 128, 128), (hi - lo + 1) * 128)]
            rhs = jnp.concatenate([text[zt, row] for row in group], axis=1)
            g = jnp.dot(lhs, rhs, preferred_element_type=F32)
            for n, row in enumerate(group):
                for y in range(lo, hi + 1):
                    if 0 <= row - y <= 6:
                        mixed[y][row - y] = diagonals(
                            lambda r: g[(y - lo) * 128 + 8 * r:(y - lo) * 128 + 8 * r + 8, n * 128:(n + 1) * 128])
        for y in range(3):
            mix = mixed[y]
            mix[7] = jnp.zeros((8, 128), F32)
            for d in (1, 2, 4):
                new = list(mix)
                keep = (lane8 & (8 * d)) == 0
                for i in range(8):
                    if not i & d:
                        a, b = mix[i], mix[i + d]
                        new[i] = jnp.where(keep, a, pltpu.roll(b, 8 * d, 1))
                        new[i + d] = jnp.where(keep, pltpu.roll(a, 128 - 8 * d, 1), b)
                mix = new
            rows = []
            for r in range(16):
                at = (16 - r) % 16
                v = mix[at % 8]
                if at >= 8:
                    v = pltpu.roll(v, 64, 1)
                keep = half
                if r in (0, 15):
                    xt = 127 - 8 * r - row8 + (lane8 & 7) - 3
                    keep = keep & (xt >= 0) & (xt < 128)
                rows.append(jnp.where(keep, v, 0.0))
            tile = (jnp.concatenate(rows, axis=0) * (128.0 ** -0.5)).astype(BF16)
            corr[pl.ds(pl.multiple_of((z * 3 + y) * 128, 128), 128), pl.ds(pl.multiple_of((zt - z) * 128, 128), 128)] = tile

    for k in range(3):
        rows_recv(0, k)

    def own(i, c):
        for zt in (3, 4, 5):
            corr_rows(i, zt)
        pass_relay(i)
        return c
    lax.fori_loop(0, 3, own, 0)
    rim_start(0, hext)

    eye = iota((96, 96), 0) == iota((96, 96), 1)

    def column(row):
        return jnp.sum(jnp.where(eye, jnp.broadcast_to(row, (96, 96)), 0.0), axis=1, keepdims=True)

    back = 127 - lane8

    def encode(z):
        acc = lax.dot_general(
            wc[...], corr[pl.ds(pl.multiple_of(z * 384, 384), 384)], (((1,), (1,)), ((), ())), preferred_element_type=F32)
        bias = column(b_enc[...])
        turned = []
        for y in range(3):
            m = motion[z, y]
            e = acc[:, y * 128:(y + 1) * 128] + bias
            for j in range(3):
                mj = jnp.take_along_axis(jnp.broadcast_to(m[j:j + 1], (8, 128)), back, axis=1, mode="promise_in_bounds")
                e = e + column(w_motion[j:j + 1]) * jnp.concatenate([mj] * 12, axis=0)
            turned.append(jnp.maximum(e, 0.0).astype(BF16))
        straight = jnp.dot(jnp.concatenate(turned, axis=0), flip, preferred_element_type=F32).astype(BF16)
        for y in range(3):
            eext[1 + z, 1 + y] = straight[y * 96:(y + 1) * 96]

    def e_rows(z, dy):
        i = 36 + z * 2 + (dy + 1) // 2
        return pltpu.make_async_remote_copy(
            src_ref=eext.at[1 + z, 2 + dy], dst_ref=eext.at[1 + z, 2 - 2 * dy],
            send_sem=rim_send.at[i], recv_sem=rim_recv.at[i], device_id=(gz, gy + dy), device_id_type=MESH)

    def e_face(dz, dy):
        i = 9 + (dz + 1) * 3 + dy + 1
        here, there = (pl.ds(1, 3), pl.ds(1, 3)) if dy == 0 else (pl.ds(2 + dy, 1), pl.ds(2 - 2 * dy, 1))
        return pltpu.make_async_remote_copy(
            src_ref=eext.at[2 + dz, here], dst_ref=eext.at[2 - 2 * dz, there],
            send_sem=rim_send.at[i], recv_sem=rim_recv.at[i], device_id=(gz + dz, gy + dy), device_id_type=MESH)

    def when_exists(dz, dy, make, act):
        @pl.when(exists(dz, dy))
        def _():
            getattr(make(), act)()

    def side_tiles(up, zu):
        z = (1 - up) * (2 - zu) + up * zu
        for k in range(zu + 1):
            corr_rows(z, (1 - up) * (2 - k) + up * (6 + k))
        return z

    for k in range(3):
        rows_recv(1, k)
    for zu in range(3):
        side_tiles(1 - odd, zu)

    @pl.when(has_relay)
    def _():
        for k in range(3):
            rows_recv(2, k)
    for zu in (2, 1, 0):
        z = side_tiles(odd, zu)
        encode(z)
        for dy in (-1, 1):
            when_exists(0, dy, lambda: e_rows(z, dy), "start")
        if zu != 1:
            dz = (zu - 1) * (2 * odd - 1)
            for dy in (0, -1, 1):
                when_exists(dz, dy, lambda: e_face(dz, dy), "start")

    def field(ref):
        cols = []
        for p in range(9):
            z, y = p // 3, p % 3
            cols.append(jnp.concatenate([ref[z + a, y + b] for a in range(3) for b in range(3)], axis=0))
        return jnp.concatenate(cols, axis=1)

    def shifted(parts, p):
        lane = iota((parts[0].shape[0], 128), 1)
        cut = slice(p * 128, (p + 1) * 128)
        left = jnp.where(lane == 0, 0.0, pltpu.roll(parts[0][:, cut], 1, 1))
        right = jnp.where(lane == 127, 0.0, pltpu.roll(parts[2][:, cut], 127, 1))
        return left + parts[1][:, cut] + right

    spread(1)
    collect(1)
    rim_recv_all(0, hext)
    ph[...] = jnp.dot(wh[0:576], field(hext), preferred_element_type=F32)
    for dy in (-1, 1):
        for z in range(3):
            when_exists(0, -dy, lambda: e_rows(z, dy), "wait_recv")
    for dz in (-1, 1):
        for dy in (-1, 0, 1):
            when_exists(-dz, -dy, lambda: e_face(dz, dy), "wait_recv")
    pe[0:288] = jnp.dot(we[0:288], field(eext), preferred_element_type=F32) + ph[0:288]

    def pick(ref, base):
        return [ref[base + c * 96:base + (c + 1) * 96] for c in range(3)]

    res_bias = column(b_res[...])
    for p in range(9):
        z, y = p // 3, p % 3
        r = jax.nn.sigmoid(shifted(pick(pe, 0), p) + res_bias)
        gext[1 + z, 1 + y] = (r * hext[1 + z, 1 + y].astype(F32)).astype(BF16)
    rim_start(2, gext)
    spread(2)
    collect(2)

    pe[288:864] = jnp.dot(we[288:864], field(eext), preferred_element_type=F32)
    for c in range(3):
        ph[288 + c * 96:288 + (c + 1) * 96] += pe[288 + c * 96:288 + (c + 1) * 96]
    upd_bias = column(b_upd[...])
    cand_bias = column(b_cand[...])
    for p in range(9):
        ph[0:96, p * 128:(p + 1) * 128] = jax.nn.sigmoid(shifted(pick(ph, 288), p) + upd_bias)
    rim_recv_all(2, gext)
    pe[0:288] = jnp.dot(wh[576:864], field(gext), preferred_element_type=F32) + pe[576:864]
    for p in range(9):
        z, y = p // 3, p % 3
        cand = jnp.tanh(shifted(pick(pe, 0), p) + cand_bias)
        u = ph[0:96, p * 128:(p + 1) * 128]
        new = ((1.0 - u) * hext[1 + z, 1 + y].astype(F32) + u * cand).astype(BF16)
        sext[:, p * 128:(p + 1) * 128] = new
        state_out[z, y] = new

    pe[0:216] = jnp.dot(whead[:, 0:96], sext[...], preferred_element_type=F32)
    for qz in (0, 4, 1, 2, 3):
        for qy in range(5):
            sums = [None] * 3
            for a in range(3):
                for b in range(3):
                    z, y = qz + a - 2, qy + b - 2
                    if 0 <= z < 3 and 0 <= y < 3:
                        for c in range(3):
                            row = ((a * 3 + b) * 3 + c) * 8
                            v = pe[row:row + 8, (z * 3 + y) * 128:(z * 3 + y + 1) * 128]
                            sums[c] = v if sums[c] is None else sums[c] + v
            left = jnp.where(lane8 == 0, 0.0, pltpu.roll(sums[0], 1, 1))
            right = jnp.where(lane8 == 127, 0.0, pltpu.roll(sums[2], 127, 1))
            hsend[qz, qy] = left + sums[1] + right

    def head_copy(d):
        dz, dy = DIRS[d]
        here = [pl.ds(1, 3) if o == 0 else pl.ds(2 + 2 * o, 1) for o in (dz, dy)]
        there = [pl.ds(0, 3) if o == 0 else pl.ds(1 - o, 1) for o in (dz, dy)]
        return pltpu.make_async_remote_copy(
            src_ref=hsend.at[here[0], here[1]], dst_ref=hrecv.at[d, there[0], there[1]],
            send_sem=rim_send.at[27 + d], recv_sem=rim_recv.at[27 + d],
            device_id=(gz + dz, gy + dy), device_id_type=MESH)

    for d, (dz, dy) in enumerate(DIRS):
        when_exists(dz, dy, lambda: head_copy(d), "start")
    for d, (dz, dy) in enumerate(DIRS):
        when_exists(-dz, -dy, lambda: head_copy(d), "wait_recv")
    for p in range(9):
        z, y = p // 3, p % 3
        out = hsend[1 + z, 1 + y]
        for d, (dz, dy) in enumerate(DIRS):
            if (dz == 0 or z == 1 - dz) and (dy == 0 or y == 1 - dy):
                out = out + hrecv[d, z, y]
        for o in range(3):
            motion_out[z, y, o:o + 1] = motion[z, y, o:o + 1] + out[o:o + 1] + b_head[0:1, o:o + 1]

    for k in range(3):
        partner_copy(k).wait_send()

        @pl.when(has_relay_dst)
        def _():
            relay_copy(k).wait_send()
        rows_sent(0, k)
        rows_sent(1, k)

        @pl.when(has_relay)
        def _():
            rows_sent(2, k)
    for rnd, ref in ((0, hext), (2, gext)):
        rim_sent(rnd, ref)
    for dy in (-1, 1):
        for z in range(3):
            when_exists(0, dy, lambda: e_rows(z, dy), "wait_send")
    for dz in (-1, 1):
        for dy in (-1, 0, 1):
            when_exists(dz, dy, lambda: e_face(dz, dy), "wait_send")
    for d, (dz, dy) in enumerate(DIRS):
        when_exists(dz, dy, lambda: head_copy(d), "wait_send")


def hand_on(a, b, c, d):
    c[...] = a[...]
    d[...] = b[...]


def solution(mesh):
    nz, ny = mesh.shape["gz"], mesh.shape["gy"]

    def on_device(source, target, hidden, motion, w_corr, w_motion, bias_encoder, w_update, bias_update, w_reset, bias_reset,
                  w_cand, bias_cand, w_head, bias_head):
        hbm = pl.BlockSpec(memory_space=pl.ANY)
        vmem = pl.BlockSpec(memory_space=pltpu.VMEM)
        ext = pltpu.VMEM((5, 5, 96, 128), BF16)
        made = pl.pallas_call(
            functools.partial(kernel, nz, ny),
            name="dvc_update",
            out_shape=(jax.ShapeDtypeStruct((3, 3, 96, 128), BF16), jax.ShapeDtypeStruct((3, 3, 3, 128), F32)),
            in_specs=[hbm, hbm, hbm, vmem, vmem, vmem, vmem, hbm, vmem, hbm, vmem, hbm, vmem, vmem, vmem],
            out_specs=(vmem, vmem),
            scratch_shapes=[
                pltpu.VMEM((3, 3, 128, 128), BF16),
                pltpu.VMEM((9, 9, 128, 128), BF16),
                ext, ext, ext,
                pltpu.VMEM((96, 1152), BF16),
                pltpu.VMEM((5, 5, 8, 128), F32), pltpu.VMEM((8, 3, 3, 8, 128), F32),
                pltpu.VMEM((3, 27, 18432), BF16),
                pltpu.VMEM((3072, 128), F32), pltpu.VMEM((3072, 128), F32),
                pltpu.VMEM((864, 864), BF16), pltpu.VMEM((864, 864), BF16),
                pltpu.VMEM((96, 896), BF16),
                pltpu.VMEM((216, 128), BF16), pltpu.VMEM((216, 128), F32),
                pltpu.VMEM((1152, 128), BF16),
                pltpu.VMEM((1152, 896), BF16),
                pltpu.VMEM((576, 1152), F32),
                pltpu.VMEM((864, 1152), F32),
                pltpu.SemaphoreType.DMA((6,)),
                pltpu.SemaphoreType.DMA((24,)), pltpu.SemaphoreType.DMA((24,)),
                pltpu.SemaphoreType.DMA((42,)), pltpu.SemaphoreType.DMA((42,)),
            ],
            compiler_params=pltpu.CompilerParams(
                collective_id=0, has_side_effects=True, vmem_limit_bytes=60 * 2 ** 20),
        )(source, target, hidden, motion, w_corr, w_motion.T, bias_encoder[None], w_update, bias_update[None], w_reset,
          bias_reset[None], w_cand, bias_cand[None], w_head.transpose(1, 0, 2), bias_head[None])
        return pl.pallas_call(
            hand_on, name="hand_on",
            out_shape=(jax.ShapeDtypeStruct((3, 3, 96, 128), BF16), jax.ShapeDtypeStruct((3, 3, 3, 128), F32)),
            in_specs=[vmem, vmem], out_specs=(vmem, vmem),
        )(*made)

    rows = P("gz", "gy", None, None)
    return jax.shard_map(
        on_device, mesh=mesh, in_specs=(rows,) * 4 + (P(),) * 11, out_specs=(rows, rows), check_vma=False)
```

```python
import functools

import jax
import jax.numpy as jnp
from jax import lax
from jax.experimental import pallas as pl
from jax.experimental.pallas import tpu as pltpu
from jax.sharding import PartitionSpec as P

MESH = pl.DeviceIdType.MESH
F32 = jnp.float32
BF16 = jnp.bfloat16
GROUPS = tuple((r,) for r in range(9))
DIRS = [(dz, dy) for dz in (-1, 0, 1) for dy in (-1, 0, 1) if (dz, dy) != (0, 0)]


def iota(shape, dim):
    return lax.broadcasted_iota(jnp.int32, shape, dim)


def kernel(nz, ny,
           src_hbm, tgt_hbm, hid_hbm, motion, w_corr, w_motion, b_enc, w_upd, b_upd, w_res, b_res, w_cand, b_cand, w_head, b_head,
           state_out, motion_out,
           src, text, hext, eext, gext, sext, hsend, hrecv, wraw, tmp_h, tmp_e, wh, we, wc, whead, headtmp, st, corr, ph, pe,
           loc_sem, blk_send, blk_recv, rim_send, rim_recv):
    gz = lax.axis_index("gz")
    gy = lax.axis_index("gy")
    odd = gz % 2
    s = 1 - 2 * odd
    has_relay_dst = (gz + 2 * s >= 0) & (gz + 2 * s < nz)
    has_relay = (gz - s >= 0) & (gz - s < nz)
    part_plane = 3 + 3 * s
    relay_plane = 3 - 3 * s

    local = []

    def fetch(a, b):
        c = pltpu.make_async_copy(a, b, loc_sem.at[len(local)])
        c.start()
        local.append(c)

    fetch(tgt_hbm, text.at[pl.ds(3, 3), pl.ds(3, 3)])
    fetch(src_hbm, src)
    fetch(hid_hbm, hext.at[pl.ds(1, 3), pl.ds(1, 3)])
    fetch(w_res, wraw.at[0])
    fetch(w_upd, wraw.at[1])
    fetch(w_cand, wraw.at[2])

    barrier = pltpu.get_barrier_semaphore()

    def exists(dz, dy):
        ok = (gz + dz >= 0) & (gz + dz < nz)
        return ok & (gy + dy >= 0) & (gy + dy < ny)

    others = DIRS + [(-2, 0), (2, 0)]
    for dz, dy in others:
        @pl.when(exists(dz, dy))
        def _():
            pl.semaphore_signal(barrier, inc=1, device_id=(gz + dz, gy + dy), device_id_type=MESH)

    for d, (dz, dy) in enumerate(DIRS):
        @pl.when(jnp.logical_not(exists(-dz, -dy)))
        def _():
            hrecv[d] = jnp.zeros((3, 3, 8, 128), F32)
    for cond, at in (
        (gz == 0, (0, None)), (gz == nz - 1, (1, None)), (gy == 0, (None, 0)), (gy == ny - 1, (None, 1)),
    ):
        @pl.when(cond)
        def _():
            if at[0] is not None:
                def zp(i, c):
                    text[6 * at[0] + i // 9, i % 9] = jnp.zeros((128, 128), BF16)
                    return c
                lax.fori_loop(0, 27, zp, 0)
                for e in (hext, eext, gext):
                    def ze(i, c):
                        e[4 * at[0], i] = jnp.zeros((96, 128), BF16)
                        return c
                    lax.fori_loop(0, 5, ze, 0)
            else:
                def zp(i, c):
                    text[i // 3, 6 * at[1] + i % 3] = jnp.zeros((128, 128), BF16)
                    return c
                lax.fori_loop(0, 27, zp, 0)
                for e in (hext, eext, gext):
                    def ze(i, c):
                        e[i, 4 * at[1]] = jnp.zeros((96, 128), BF16)
                        return c
                    lax.fori_loop(0, 5, ze, 0)

    lane8 = iota((8, 128), 1)
    row8 = iota((8, 128), 0)
    flip = jnp.where(iota((128, 128), 0) + iota((128, 128), 1) == 127, 1.0, 0.0).astype(BF16)

    for a in range(7):
        kk = iota((343, 128), 1)
        want = a * 49 + (kk // 8) * 7 + kk % 8
        pick = (iota((343, 128), 0) == want) & (kk % 8 < 7) & (kk < 56)
        wc[:, a * 128:(a + 1) * 128] = jnp.dot(
            w_corr[...], jnp.where(pick, 1.0, 0.0).astype(BF16), preferred_element_type=F32).astype(BF16)

    local[1].wait()

    for p in range(9):
        st[p * 128:(p + 1) * 128] = lax.dot_general(
            flip, src[p // 3, p % 3], (((1,), (1,)), ((), ())), preferred_element_type=F32).astype(BF16)

    headtmp[...] = jnp.zeros_like(headtmp)
    for o in range(3):
        headtmp[pl.ds(o, 27, stride=8), :] = jnp.concatenate([w_head[o].astype(F32), jnp.zeros((27, 32), F32)], axis=1)
    whead[...] = headtmp[...].astype(BF16)

    local[0].wait()
    local[2].wait()
    zs = sum((d + nz - 1) // nz for d in (gz, nz - 1 - gz))
    ys = sum((d + ny - 1) // ny for d in (gy, ny - 1 - gy))
    zs2 = sum((d + nz - 2) // nz for d in (gz, nz - 1 - gz))
    pl.semaphore_wait(barrier, (1 + zs) * (1 + ys) - 1 + zs2)

    def partner_copy(k):
        return pltpu.make_async_remote_copy(
            src_ref=text.at[3 + k, pl.ds(3, 3)], dst_ref=text.at[relay_plane + k, pl.ds(3, 3)],
            send_sem=blk_send.at[k], recv_sem=blk_recv.at[k],
            device_id=(gz + s, gy), device_id_type=MESH)

    def relay_copy(k):
        return pltpu.make_async_remote_copy(
            src_ref=text.at[part_plane + k, pl.ds(3, 3)], dst_ref=text.at[relay_plane + k, pl.ds(3, 3)],
            send_sem=blk_send.at[3 + k], recv_sem=blk_recv.at[3 + k],
            device_id=(gz + 2 * s, gy), device_id_type=MESH)

    def row_copy(group, k, side):
        plane = (3, part_plane, relay_plane)[group] + k
        i = 6 + (group * 3 + k) * 2 + side
        return pltpu.make_async_remote_copy(
            src_ref=text.at[plane, pl.ds(3, 3)], dst_ref=text.at[plane, pl.ds(6 - 6 * side, 3)],
            send_sem=blk_send.at[i], recv_sem=blk_recv.at[i],
            device_id=(gz, gy + 2 * side - 1), device_id_type=MESH)

    side_ok = (gy > 0, gy < ny - 1)
    mid = ny // 2
    cross = (gy == mid, gy == mid - 1)
    at_cross = cross[0] | cross[1]
    far = 6 * (mid - gy)

    def open_side(group, side):
        return side_ok[side] if group == 0 else side_ok[side] & jnp.logical_not(cross[side])

    def far_partner(k):
        return pltpu.make_async_remote_copy(
            src_ref=text.at[3 + k, pl.ds(far, 3)], dst_ref=text.at[relay_plane + k, pl.ds(far, 3)],
            send_sem=blk_send.at[24 + k], recv_sem=blk_recv.at[24 + k],
            device_id=(gz + s, gy), device_id_type=MESH)

    def far_relay(k):
        return pltpu.make_async_remote_copy(
            src_ref=text.at[part_plane + k, pl.ds(far, 3)], dst_ref=text.at[relay_plane + k, pl.ds(far, 3)],
            send_sem=blk_send.at[27 + k], recv_sem=blk_recv.at[27 + k],
            device_id=(gz + 2 * s, gy), device_id_type=MESH)

    def rows_start(group, k):
        for side in (0, 1):
            @pl.when(open_side(group, side))
            def _():
                row_copy(group, k, side).start()

    def rows_recv(group, k):
        for side in (0, 1):
            @pl.when(open_side(group, 1 - side))
            def _():
                row_copy(group, k, side).wait_recv()

    def rows_sent(group, k):
        for side in (0, 1):
            @pl.when(open_side(group, side))
            def _():
                row_copy(group, k, side).wait_send()

    for k in range(3):
        partner_copy(k).start()
        rows_start(0, k)

    def rim_copy(rnd, ref, d):
        dz, dy = DIRS[d]

        def sl(o, here):
            if o == 0:
                return pl.ds(1, 3)
            return pl.ds((3 if o > 0 else 1) if here else (0 if o > 0 else 4), 1)
        return pltpu.make_async_remote_copy(
            src_ref=ref.at[sl(dz, True), sl(dy, True)], dst_ref=ref.at[sl(dz, False), sl(dy, False)],
            send_sem=rim_send.at[rnd * 9 + d], recv_sem=rim_recv.at[rnd * 9 + d],
            device_id=(gz + dz, gy + dy), device_id_type=MESH)

    def rim_start(rnd, ref):
        for d, (dz, dy) in enumerate(DIRS):
            @pl.when(exists(dz, dy))
            def _():
                rim_copy(rnd, ref, d).start()

    def rim_recv_all(rnd, ref):
        for d, (dz, dy) in enumerate(DIRS):
            @pl.when(exists(-dz, -dy))
            def _():
                rim_copy(rnd, ref, d).wait_recv()

    def rim_sent(rnd, ref):
        for d, (dz, dy) in enumerate(DIRS):
            @pl.when(exists(dz, dy))
            def _():
                rim_copy(rnd, ref, d).wait_send()

    def spread(w):
        local[3 + w].wait()

        def some(op4, c):
            for u in range(4):
                op = op4 * 4 + u
                x = wraw[w, :, pl.ds(pl.multiple_of(op * 384, 384), 384)].astype(F32)
                r = pl.multiple_of(op * 64, 64)
                tmp_h[pl.ds(r, 27), 0:96] = x[:, 0:96]
                tmp_e[pl.ds(r, 27), 0:96] = x[:, 96:192]
                tmp_h[pl.ds(r + 32, 27), 0:96] = x[:, 192:288]
                tmp_e[pl.ds(r + 32, 27), 0:96] = x[:, 288:384]
            return c
        lax.fori_loop(0, 12, some, 0)

    def collect(w):
        for tmp, dst in ((tmp_h, wh), (tmp_e, we)):
            for ab in range(9):
                for c in range(3):
                    v = tmp[pl.ds(ab * 3 + c, 96, stride=32), :]
                    row = w * 288 + c * 96
                    dst[row:row + 96, ab * 96:(ab + 1) * 96] = v[:, 0:96].astype(BF16)

    def pass_partner(k):
        partner_copy(k).wait_recv()

        @pl.when(has_relay_dst)
        def _():
            relay_copy(k).start()
        rows_start(1, k)

    def pass_relay(k):
        @pl.when(has_relay)
        def _():
            relay_copy(k).wait_recv()
            rows_start(2, k)

    spread(0)
    pass_partner(0)
    collect(0)
    pass_partner(1)
    pass_partner(2)

    half = lane8 < 64

    def corr_rows(z, zt):
        mixed = [[None] * 8 for _ in range(3)]

        def diagonals(g):
            skewed = []
            for par in range(2):
                v = g(par)
                for r in range(par + 2, 16, 2):
                    v = jnp.where(lane8 < 132 - 8 * r, g(r), v)
                skewed.append(pltpu.roll(v, 4, 1, stride=1, stride_axis=0))
            return jnp.where((lane8 & 8) == 0, skewed[0], skewed[1])

        for group in GROUPS:
            lo = max(0, min(group) - 6)
            hi = min(2, max(group))
            lhs = st[pl.ds(pl.multiple_of((z * 3 + lo) * 128, 128), (hi - lo + 1) * 128)]
            rhs = jnp.concatenate([text[zt, row] for row in group], axis=1)
            g = jnp.dot(lhs, rhs, preferred_element_type=F32)
            for n, row in enumerate(group):
                for y in range(lo, hi + 1):
                    if 0 <= row - y <= 6:
                        mixed[y][row - y] = diagonals(
                            lambda r: g[(y - lo) * 128 + 8 * r:(y - lo) * 128 + 8 * r + 8, n * 128:(n + 1) * 128])
        for y in range(3):
            mix = mixed[y]
            mix[7] = jnp.zeros((8, 128), F32)
            for d in (1, 2, 4):
                new = list(mix)
                keep = (lane8 & (8 * d)) == 0
                for i in range(8):
                    if not i & d:
                        a, b = mix[i], mix[i + d]
                        new[i] = jnp.where(keep, a, pltpu.roll(b, 8 * d, 1))
                        new[i + d] = jnp.where(keep, pltpu.roll(a, 128 - 8 * d, 1), b)
                mix = new
            rows = []
            for r in range(16):
                at = (16 - r) % 16
                v = mix[at % 8]
                if at >= 8:
                    v = pltpu.roll(v, 64, 1)
                keep = half
                if r in (0, 15):
                    xt = 127 - 8 * r - row8 + (lane8 & 7) - 3
                    keep = keep & (xt >= 0) & (xt < 128)
                rows.append(jnp.where(keep, v, 0.0))
            tile = (jnp.concatenate(rows, axis=0) * (128.0 ** -0.5)).astype(BF16)
            corr[pl.ds(pl.multiple_of((z * 3 + y) * 128, 128), 128), pl.ds(pl.multiple_of((zt - z) * 128, 128), 128)] = tile

    for k in range(3):
        rows_recv(0, k)

        @pl.when(at_cross)
        def _():
            far_partner(k).start()

    def own(i, c):
        for zt in (3, 4, 5):
            corr_rows(i, zt)
        pass_relay(i)

        @pl.when(at_cross)
        def _():
            far_partner(i).wait_recv()

            @pl.when(has_relay_dst)
            def _():
                far_relay(i).start()
        return c
    lax.fori_loop(0, 3, own, 0)
    rim_start(0, hext)

    eye = iota((96, 96), 0) == iota((96, 96), 1)

    def column(row):
        return jnp.sum(jnp.where(eye, jnp.broadcast_to(row, (96, 96)), 0.0), axis=1, keepdims=True)

    back = 127 - lane8

    def encode(z):
        acc = lax.dot_general(
            wc[...], corr[pl.ds(pl.multiple_of(z * 384, 384), 384)], (((1,), (1,)), ((), ())), preferred_element_type=F32)
        bias = column(b_enc[...])
        turned = []
        for y in range(3):
            m = motion[z, y]
            e = acc[:, y * 128:(y + 1) * 128] + bias
            for j in range(3):
                mj = jnp.take_along_axis(jnp.broadcast_to(m[j:j + 1], (8, 128)), back, axis=1, mode="promise_in_bounds")
                e = e + column(w_motion[j:j + 1]) * jnp.concatenate([mj] * 12, axis=0)
            turned.append(jnp.maximum(e, 0.0).astype(BF16))
        straight = jnp.dot(jnp.concatenate(turned, axis=0), flip, preferred_element_type=F32).astype(BF16)
        for y in range(3):
            eext[1 + z, 1 + y] = straight[y * 96:(y + 1) * 96]

    def e_rows(z, dy):
        i = 36 + z * 2 + (dy + 1) // 2
        return pltpu.make_async_remote_copy(
            src_ref=eext.at[1 + z, 2 + dy], dst_ref=eext.at[1 + z, 2 - 2 * dy],
            send_sem=rim_send.at[i], recv_sem=rim_recv.at[i], device_id=(gz, gy + dy), device_id_type=MESH)

    def e_face(dz, dy):
        i = 9 + (dz + 1) * 3 + dy + 1
        here, there = (pl.ds(1, 3), pl.ds(1, 3)) if dy == 0 else (pl.ds(2 + dy, 1), pl.ds(2 - 2 * dy, 1))
        return pltpu.make_async_remote_copy(
            src_ref=eext.at[2 + dz, here], dst_ref=eext.at[2 - 2 * dz, there],
            send_sem=rim_send.at[i], recv_sem=rim_recv.at[i], device_id=(gz + dz, gy + dy), device_id_type=MESH)

    def when_exists(dz, dy, make, act):
        @pl.when(exists(dz, dy))
        def _():
            getattr(make(), act)()

    def side_tiles(up, zu):
        z = (1 - up) * (2 - zu) + up * zu
        for k in range(zu + 1):
            corr_rows(z, (1 - up) * (2 - k) + up * (6 + k))
        return z

    for k in range(3):
        rows_recv(1, k)
    for zu in range(3):
        side_tiles(1 - odd, zu)

    @pl.when(has_relay)
    def _():
        for k in range(3):
            rows_recv(2, k)

            @pl.when(at_cross)
            def _():
                far_relay(k).wait_recv()
    for zu in (2, 1, 0):
        z = side_tiles(odd, zu)
        encode(z)
        for dy in (-1, 1):
            when_exists(0, dy, lambda: e_rows(z, dy), "start")
        if zu != 1:
            dz = (zu - 1) * (2 * odd - 1)
            for dy in (0, -1, 1):
                when_exists(dz, dy, lambda: e_face(dz, dy), "start")

    def field(ref):
        cols = []
        for p in range(9):
            z, y = p // 3, p % 3
            cols.append(jnp.concatenate([ref[z + a, y + b] for a in range(3) for b in range(3)], axis=0))
        return jnp.concatenate(cols, axis=1)

    def shifted(parts, p):
        lane = iota((parts[0].shape[0], 128), 1)
        cut = slice(p * 128, (p + 1) * 128)
        left = jnp.where(lane == 0, 0.0, pltpu.roll(parts[0][:, cut], 1, 1))
        right = jnp.where(lane == 127, 0.0, pltpu.roll(parts[2][:, cut], 127, 1))
        return left + parts[1][:, cut] + right

    spread(1)
    collect(1)
    rim_recv_all(0, hext)
    ph[...] = jnp.dot(wh[0:576], field(hext), preferred_element_type=F32)
    for dy in (-1, 1):
        for z in range(3):
            when_exists(0, -dy, lambda: e_rows(z, dy), "wait_recv")
    for dz in (-1, 1):
        for dy in (-1, 0, 1):
            when_exists(-dz, -dy, lambda: e_face(dz, dy), "wait_recv")
    pe[0:288] = jnp.dot(we[0:288], field(eext), preferred_element_type=F32) + ph[0:288]

    def pick(ref, base):
        return [ref[base + c * 96:base + (c + 1) * 96] for c in range(3)]

    res_bias = column(b_res[...])
    for p in range(9):
        z, y = p // 3, p % 3
        r = jax.nn.sigmoid(shifted(pick(pe, 0), p) + res_bias)
        gext[1 + z, 1 + y] = (r * hext[1 + z, 1 + y].astype(F32)).astype(BF16)
    rim_start(2, gext)
    spread(2)
    collect(2)

    pe[288:864] = jnp.dot(we[288:864], field(eext), preferred_element_type=F32)
    for c in range(3):
        ph[288 + c * 96:288 + (c + 1) * 96] += pe[288 + c * 96:288 + (c + 1) * 96]
    upd_bias = column(b_upd[...])
    cand_bias = column(b_cand[...])
    for p in range(9):
        ph[0:96, p * 128:(p + 1) * 128] = jax.nn.sigmoid(shifted(pick(ph, 288), p) + upd_bias)
    rim_recv_all(2, gext)
    pe[0:288] = jnp.dot(wh[576:864], field(gext), preferred_element_type=F32) + pe[576:864]
    for p in range(9):
        z, y = p // 3, p % 3
        cand = jnp.tanh(shifted(pick(pe, 0), p) + cand_bias)
        u = ph[0:96, p * 128:(p + 1) * 128]
        new = ((1.0 - u) * hext[1 + z, 1 + y].astype(F32) + u * cand).astype(BF16)
        sext[:, p * 128:(p + 1) * 128] = new
        state_out[z, y] = new

    pe[0:216] = jnp.dot(whead[:, 0:96], sext[...], preferred_element_type=F32)
    for qz in (0, 4, 1, 2, 3):
        for qy in range(5):
            sums = [None] * 3
            for a in range(3):
                for b in range(3):
                    z, y = qz + a - 2, qy + b - 2
                    if 0 <= z < 3 and 0 <= y < 3:
                        for c in range(3):
                            row = ((a * 3 + b) * 3 + c) * 8
                            v = pe[row:row + 8, (z * 3 + y) * 128:(z * 3 + y + 1) * 128]
                            sums[c] = v if sums[c] is None else sums[c] + v
            left = jnp.where(lane8 == 0, 0.0, pltpu.roll(sums[0], 1, 1))
            right = jnp.where(lane8 == 127, 0.0, pltpu.roll(sums[2], 127, 1))
            hsend[qz, qy] = left + sums[1] + right

    def head_copy(d):
        dz, dy = DIRS[d]
        here = [pl.ds(1, 3) if o == 0 else pl.ds(2 + 2 * o, 1) for o in (dz, dy)]
        there = [pl.ds(0, 3) if o == 0 else pl.ds(1 - o, 1) for o in (dz, dy)]
        return pltpu.make_async_remote_copy(
            src_ref=hsend.at[here[0], here[1]], dst_ref=hrecv.at[d, there[0], there[1]],
            send_sem=rim_send.at[27 + d], recv_sem=rim_recv.at[27 + d],
            device_id=(gz + dz, gy + dy), device_id_type=MESH)

    for d, (dz, dy) in enumerate(DIRS):
        when_exists(dz, dy, lambda: head_copy(d), "start")
    for d, (dz, dy) in enumerate(DIRS):
        when_exists(-dz, -dy, lambda: head_copy(d), "wait_recv")
    for p in range(9):
        z, y = p // 3, p % 3
        out = hsend[1 + z, 1 + y]
        for d, (dz, dy) in enumerate(DIRS):
            if (dz == 0 or z == 1 - dz) and (dy == 0 or y == 1 - dy):
                out = out + hrecv[d, z, y]
        for o in range(3):
            motion_out[z, y, o:o + 1] = motion[z, y, o:o + 1] + out[o:o + 1] + b_head[0:1, o:o + 1]

    for k in range(3):
        partner_copy(k).wait_send()

        @pl.when(has_relay_dst)
        def _():
            relay_copy(k).wait_send()
        rows_sent(0, k)
        rows_sent(1, k)

        @pl.when(has_relay)
        def _():
            rows_sent(2, k)

        @pl.when(at_cross)
        def _():
            far_partner(k).wait_send()

            @pl.when(has_relay_dst)
            def _():
                far_relay(k).wait_send()
    for rnd, ref in ((0, hext), (2, gext)):
        rim_sent(rnd, ref)
    for dy in (-1, 1):
        for z in range(3):
            when_exists(0, dy, lambda: e_rows(z, dy), "wait_send")
    for dz in (-1, 1):
        for dy in (-1, 0, 1):
            when_exists(dz, dy, lambda: e_face(dz, dy), "wait_send")
    for d, (dz, dy) in enumerate(DIRS):
        when_exists(dz, dy, lambda: head_copy(d), "wait_send")


def hand_on(a, b, c, d):
    c[...] = a[...]
    d[...] = b[...]


def solution(mesh):
    nz, ny = mesh.shape["gz"], mesh.shape["gy"]

    def on_device(source, target, hidden, motion, w_corr, w_motion, bias_encoder, w_update, bias_update, w_reset, bias_reset,
                  w_cand, bias_cand, w_head, bias_head):
        hbm = pl.BlockSpec(memory_space=pl.ANY)
        vmem = pl.BlockSpec(memory_space=pltpu.VMEM)
        ext = pltpu.VMEM((5, 5, 96, 128), BF16)
        made = pl.pallas_call(
            functools.partial(kernel, nz, ny),
            name="dvc_update",
            out_shape=(jax.ShapeDtypeStruct((3, 3, 96, 128), BF16), jax.ShapeDtypeStruct((3, 3, 3, 128), F32)),
            in_specs=[hbm, hbm, hbm, vmem, vmem, vmem, vmem, hbm, vmem, hbm, vmem, hbm, vmem, vmem, vmem],
            out_specs=(vmem, vmem),
            scratch_shapes=[
                pltpu.VMEM((3, 3, 128, 128), BF16),
                pltpu.VMEM((9, 9, 128, 128), BF16),
                ext, ext, ext,
                pltpu.VMEM((96, 1152), BF16),
                pltpu.VMEM((5, 5, 8, 128), F32), pltpu.VMEM((8, 3, 3, 8, 128), F32),
                pltpu.VMEM((3, 27, 18432), BF16),
                pltpu.VMEM((3072, 128), F32), pltpu.VMEM((3072, 128), F32),
                pltpu.VMEM((864, 864), BF16), pltpu.VMEM((864, 864), BF16),
                pltpu.VMEM((96, 896), BF16),
                pltpu.VMEM((216, 128), BF16), pltpu.VMEM((216, 128), F32),
                pltpu.VMEM((1152, 128), BF16),
                pltpu.VMEM((1152, 896), BF16),
                pltpu.VMEM((576, 1152), F32),
                pltpu.VMEM((864, 1152), F32),
                pltpu.SemaphoreType.DMA((6,)),
                pltpu.SemaphoreType.DMA((30,)), pltpu.SemaphoreType.DMA((30,)),
                pltpu.SemaphoreType.DMA((42,)), pltpu.SemaphoreType.DMA((42,)),
            ],
            compiler_params=pltpu.CompilerParams(
                collective_id=0, has_side_effects=True, vmem_limit_bytes=60 * 2 ** 20),
        )(source, target, hidden, motion, w_corr, w_motion.T, bias_encoder[None], w_update, bias_update[None], w_reset,
          bias_reset[None], w_cand, bias_cand[None], w_head.transpose(1, 0, 2), bias_head[None])
        return pl.pallas_call(
            hand_on, name="hand_on",
            out_shape=(jax.ShapeDtypeStruct((3, 3, 96, 128), BF16), jax.ShapeDtypeStruct((3, 3, 3, 128), F32)),
            in_specs=[vmem, vmem], out_specs=(vmem, vmem),
        )(*made)

    rows = P("gz", "gy", None, None)
    return jax.shard_map(
        on_device, mesh=mesh, in_specs=(rows,) * 4 + (P(),) * 11, out_specs=(rows, rows), check_vma=False)
```

```python
import functools

import jax
import jax.numpy as jnp
from jax import lax
from jax.experimental import pallas as pl
from jax.experimental.pallas import tpu as pltpu
from jax.sharding import PartitionSpec as P

MESH = pl.DeviceIdType.MESH
F32 = jnp.float32
BF16 = jnp.bfloat16
GROUPS = tuple((r,) for r in range(9))
DIRS = [(dz, dy) for dz in (-1, 0, 1) for dy in (-1, 0, 1) if (dz, dy) != (0, 0)]


def iota(shape, dim):
    return lax.broadcasted_iota(jnp.int32, shape, dim)


def kernel(nz, ny,
           src_hbm, tgt_hbm, hid_hbm, motion, w_corr, w_motion, b_enc, w_upd, b_upd, w_res, b_res, w_cand, b_cand, w_head, b_head,
           state_out, motion_out,
           src, text, hext, eext, gext, sext, hsend, hrecv, wraw, tmp_h, tmp_e, wh, we, wc, whead, headtmp, st, corr, ph, pe,
           loc_sem, blk_send, blk_recv, rim_send, rim_recv):
    gz = lax.axis_index("gz")
    gy = lax.axis_index("gy")
    odd = gz % 2
    s = 1 - 2 * odd
    has_relay_dst = (gz + 2 * s >= 0) & (gz + 2 * s < nz)
    has_relay = (gz - s >= 0) & (gz - s < nz)
    part_plane = 3 + 3 * s
    relay_plane = 3 - 3 * s

    local = []

    def fetch(a, b):
        c = pltpu.make_async_copy(a, b, loc_sem.at[len(local)])
        c.start()
        local.append(c)

    fetch(tgt_hbm, text.at[pl.ds(3, 3), pl.ds(3, 3)])
    fetch(src_hbm, src)
    fetch(hid_hbm, hext.at[pl.ds(1, 3), pl.ds(1, 3)])
    fetch(w_res, wraw.at[0])
    fetch(w_upd, wraw.at[1])
    fetch(w_cand, wraw.at[2])

    barrier = pltpu.get_barrier_semaphore()

    def exists(dz, dy):
        ok = (gz + dz >= 0) & (gz + dz < nz)
        return ok & (gy + dy >= 0) & (gy + dy < ny)

    others = DIRS + [(-2, 0), (2, 0)]
    for dz, dy in others:
        @pl.when(exists(dz, dy))
        def _():
            pl.semaphore_signal(barrier, inc=1, device_id=(gz + dz, gy + dy), device_id_type=MESH)

    for d, (dz, dy) in enumerate(DIRS):
        @pl.when(jnp.logical_not(exists(-dz, -dy)))
        def _():
            hrecv[d] = jnp.zeros((3, 3, 8, 128), F32)
    for cond, at in (
        (gz == 0, (0, None)), (gz == nz - 1, (1, None)), (gy == 0, (None, 0)), (gy == ny - 1, (None, 1)),
    ):
        @pl.when(cond)
        def _():
            if at[0] is not None:
                def zp(i, c):
                    text[6 * at[0] + i // 9, i % 9] = jnp.zeros((128, 128), BF16)
                    return c
                lax.fori_loop(0, 27, zp, 0)
                for e in (hext, eext, gext):
                    def ze(i, c):
                        e[4 * at[0], i] = jnp.zeros((96, 128), BF16)
                        return c
                    lax.fori_loop(0, 5, ze, 0)
            else:
                def zp(i, c):
                    text[i // 3, 6 * at[1] + i % 3] = jnp.zeros((128, 128), BF16)
                    return c
                lax.fori_loop(0, 27, zp, 0)
                for e in (hext, eext, gext):
                    def ze(i, c):
                        e[i, 4 * at[1]] = jnp.zeros((96, 128), BF16)
                        return c
                    lax.fori_loop(0, 5, ze, 0)

    lane8 = iota((8, 128), 1)
    row8 = iota((8, 128), 0)
    flip = jnp.where(iota((128, 128), 0) + iota((128, 128), 1) == 127, 1.0, 0.0).astype(BF16)

    for a in range(7):
        kk = iota((343, 128), 1)
        want = a * 49 + (kk // 8) * 7 + kk % 8
        pick = (iota((343, 128), 0) == want) & (kk % 8 < 7) & (kk < 56)
        wc[:, a * 128:(a + 1) * 128] = jnp.dot(
            w_corr[...], jnp.where(pick, 1.0, 0.0).astype(BF16), preferred_element_type=F32).astype(BF16)

    local[1].wait()

    for p in range(9):
        st[p * 128:(p + 1) * 128] = lax.dot_general(
            flip, src[p // 3, p % 3], (((1,), (1,)), ((), ())), preferred_element_type=F32).astype(BF16)

    headtmp[...] = jnp.zeros_like(headtmp)
    for o in range(3):
        headtmp[pl.ds(o, 27, stride=8), :] = jnp.concatenate([w_head[o].astype(F32), jnp.zeros((27, 32), F32)], axis=1)
    whead[...] = headtmp[...].astype(BF16)

    local[0].wait()
    local[2].wait()
    zs = sum((d + nz - 1) // nz for d in (gz, nz - 1 - gz))
    ys = sum((d + ny - 1) // ny for d in (gy, ny - 1 - gy))
    zs2 = sum((d + nz - 2) // nz for d in (gz, nz - 1 - gz))
    pl.semaphore_wait(barrier, (1 + zs) * (1 + ys) - 1 + zs2)

    def partner_copy(k):
        return pltpu.make_async_remote_copy(
            src_ref=text.at[3 + k, pl.ds(3, 3)], dst_ref=text.at[relay_plane + k, pl.ds(3, 3)],
            send_sem=blk_send.at[k], recv_sem=blk_recv.at[k],
            device_id=(gz + s, gy), device_id_type=MESH)

    def relay_copy(k):
        return pltpu.make_async_remote_copy(
            src_ref=text.at[part_plane + k, pl.ds(3, 3)], dst_ref=text.at[relay_plane + k, pl.ds(3, 3)],
            send_sem=blk_send.at[3 + k], recv_sem=blk_recv.at[3 + k],
            device_id=(gz + 2 * s, gy), device_id_type=MESH)

    def row_copy(group, k, side):
        plane = (3, part_plane, relay_plane)[group] + k
        i = 6 + (group * 3 + k) * 2 + side
        return pltpu.make_async_remote_copy(
            src_ref=text.at[plane, pl.ds(3, 3)], dst_ref=text.at[plane, pl.ds(6 - 6 * side, 3)],
            send_sem=blk_send.at[i], recv_sem=blk_recv.at[i],
            device_id=(gz, gy + 2 * side - 1), device_id_type=MESH)

    side_ok = (gy > 0, gy < ny - 1)
    mid = ny // 2
    cross = (gy == mid, gy == mid - 1)
    at_cross = cross[0] | cross[1]
    far = 6 * (mid - gy)

    def open_side(group, side):
        return side_ok[side] if group == 0 else side_ok[side] & jnp.logical_not(cross[side])

    def far_partner(k):
        return pltpu.make_async_remote_copy(
            src_ref=text.at[3 + k, pl.ds(far, 3)], dst_ref=text.at[relay_plane + k, pl.ds(far, 3)],
            send_sem=blk_send.at[24 + k], recv_sem=blk_recv.at[24 + k],
            device_id=(gz + s, gy), device_id_type=MESH)

    def far_relay(k):
        return pltpu.make_async_remote_copy(
            src_ref=text.at[part_plane + k, pl.ds(far, 3)], dst_ref=text.at[relay_plane + k, pl.ds(far, 3)],
            send_sem=blk_send.at[27 + k], recv_sem=blk_recv.at[27 + k],
            device_id=(gz + 2 * s, gy), device_id_type=MESH)

    def rows_start(group, k):
        for side in (0, 1):
            @pl.when(open_side(group, side))
            def _():
                row_copy(group, k, side).start()

    def rows_recv(group, k):
        for side in (0, 1):
            @pl.when(open_side(group, 1 - side))
            def _():
                row_copy(group, k, side).wait_recv()

    def rows_sent(group, k):
        for side in (0, 1):
            @pl.when(open_side(group, side))
            def _():
                row_copy(group, k, side).wait_send()

    for k in range(3):
        partner_copy(k).start()
        rows_start(0, k)

    def rim_copy(rnd, ref, d):
        dz, dy = DIRS[d]

        def sl(o, here):
            if o == 0:
                return pl.ds(1, 3)
            return pl.ds((3 if o > 0 else 1) if here else (0 if o > 0 else 4), 1)
        return pltpu.make_async_remote_copy(
            src_ref=ref.at[sl(dz, True), sl(dy, True)], dst_ref=ref.at[sl(dz, False), sl(dy, False)],
            send_sem=rim_send.at[rnd * 9 + d], recv_sem=rim_recv.at[rnd * 9 + d],
            device_id=(gz + dz, gy + dy), device_id_type=MESH)

    def rim_start(rnd, ref):
        for d, (dz, dy) in enumerate(DIRS):
            @pl.when(exists(dz, dy))
            def _():
                rim_copy(rnd, ref, d).start()

    def rim_recv_all(rnd, ref):
        for d, (dz, dy) in enumerate(DIRS):
            @pl.when(exists(-dz, -dy))
            def _():
                rim_copy(rnd, ref, d).wait_recv()

    def rim_sent(rnd, ref):
        for d, (dz, dy) in enumerate(DIRS):
            @pl.when(exists(dz, dy))
            def _():
                rim_copy(rnd, ref, d).wait_send()

    def spread(w):
        local[3 + w].wait()

        def some(op4, c):
            for u in range(4):
                op = op4 * 4 + u
                x = wraw[w, :, pl.ds(pl.multiple_of(op * 384, 384), 384)].astype(F32)
                r = pl.multiple_of(op * 64, 64)
                tmp_h[pl.ds(r, 27), 0:96] = x[:, 0:96]
                tmp_e[pl.ds(r, 27), 0:96] = x[:, 96:192]
                tmp_h[pl.ds(r + 32, 27), 0:96] = x[:, 192:288]
                tmp_e[pl.ds(r + 32, 27), 0:96] = x[:, 288:384]
            return c
        lax.fori_loop(0, 12, some, 0)

    def collect(w):
        for tmp, dst in ((tmp_h, wh), (tmp_e, we)):
            for ab in range(9):
                for c in range(3):
                    v = tmp[pl.ds(ab * 3 + c, 96, stride=32), :]
                    row = w * 288 + c * 96
                    dst[row:row + 96, ab * 96:(ab + 1) * 96] = v[:, 0:96].astype(BF16)

    def pass_partner(k):
        partner_copy(k).wait_recv()

        @pl.when(has_relay_dst)
        def _():
            relay_copy(k).start()
        rows_start(1, k)

    def pass_relay(k):
        @pl.when(has_relay)
        def _():
            relay_copy(k).wait_recv()
            rows_start(2, k)

    spread(0)
    pass_partner(0)
    collect(0)
    pass_partner(1)
    spread(1)
    pass_partner(2)

    half = lane8 < 64

    def corr_rows(z, zt):
        mixed = [[None] * 8 for _ in range(3)]

        def diagonals(g):
            skewed = []
            for par in range(2):
                v = g(par)
                for r in range(par + 2, 16, 2):
                    v = jnp.where(lane8 < 132 - 8 * r, g(r), v)
                skewed.append(pltpu.roll(v, 4, 1, stride=1, stride_axis=0))
            return jnp.where((lane8 & 8) == 0, skewed[0], skewed[1])

        for group in GROUPS:
            lo = max(0, min(group) - 6)
            hi = min(2, max(group))
            lhs = st[pl.ds(pl.multiple_of((z * 3 + lo) * 128, 128), (hi - lo + 1) * 128)]
            rhs = jnp.concatenate([text[zt, row] for row in group], axis=1)
            g = jnp.dot(lhs, rhs, preferred_element_type=F32)
            for n, row in enumerate(group):
                for y in range(lo, hi + 1):
                    if 0 <= row - y <= 6:
                        mixed[y][row - y] = diagonals(
                            lambda r: g[(y - lo) * 128 + 8 * r:(y - lo) * 128 + 8 * r + 8, n * 128:(n + 1) * 128])
        for y in range(3):
            mix = mixed[y]
            mix[7] = jnp.zeros((8, 128), F32)
            for d in (1, 2, 4):
                new = list(mix)
                keep = (lane8 & (8 * d)) == 0
                for i in range(8):
                    if not i & d:
                        a, b = mix[i], mix[i + d]
                        new[i] = jnp.where(keep, a, pltpu.roll(b, 8 * d, 1))
                        new[i + d] = jnp.where(keep, pltpu.roll(a, 128 - 8 * d, 1), b)
                mix = new
            rows = []
            for r in range(16):
                at = (16 - r) % 16
                v = mix[at % 8]
                if at >= 8:
                    v = pltpu.roll(v, 64, 1)
                keep = half
                if r in (0, 15):
                    xt = 127 - 8 * r - row8 + (lane8 & 7) - 3
                    keep = keep & (xt >= 0) & (xt < 128)
                rows.append(jnp.where(keep, v, 0.0))
            tile = (jnp.concatenate(rows, axis=0) * (128.0 ** -0.5)).astype(BF16)
            corr[pl.ds(pl.multiple_of((z * 3 + y) * 128, 128), 128), pl.ds(pl.multiple_of((zt - z) * 128, 128), 128)] = tile

    for k in range(3):
        rows_recv(0, k)

        @pl.when(at_cross)
        def _():
            far_partner(k).start()

    def own(i, c):
        for zt in (3, 4, 5):
            corr_rows(i, zt)
        pass_relay(i)

        @pl.when(at_cross)
        def _():
            far_partner(i).wait_recv()

            @pl.when(has_relay_dst)
            def _():
                far_relay(i).start()
        return c
    lax.fori_loop(0, 3, own, 0)
    rim_start(0, hext)

    eye = iota((96, 96), 0) == iota((96, 96), 1)

    def column(row):
        return jnp.sum(jnp.where(eye, jnp.broadcast_to(row, (96, 96)), 0.0), axis=1, keepdims=True)

    back = 127 - lane8

    def encode(z):
        acc = lax.dot_general(
            wc[...], corr[pl.ds(pl.multiple_of(z * 384, 384), 384)], (((1,), (1,)), ((), ())), preferred_element_type=F32)
        bias = column(b_enc[...])
        turned = []
        for y in range(3):
            m = motion[z, y]
            e = acc[:, y * 128:(y + 1) * 128] + bias
            for j in range(3):
                mj = jnp.take_along_axis(jnp.broadcast_to(m[j:j + 1], (8, 128)), back, axis=1, mode="promise_in_bounds")
                e = e + column(w_motion[j:j + 1]) * jnp.concatenate([mj] * 12, axis=0)
            turned.append(jnp.maximum(e, 0.0).astype(BF16))
        straight = jnp.dot(jnp.concatenate(turned, axis=0), flip, preferred_element_type=F32).astype(BF16)
        for y in range(3):
            eext[1 + z, 1 + y] = straight[y * 96:(y + 1) * 96]

    def e_rows(z, dy):
        i = 36 + z * 2 + (dy + 1) // 2
        return pltpu.make_async_remote_copy(
            src_ref=eext.at[1 + z, 2 + dy], dst_ref=eext.at[1 + z, 2 - 2 * dy],
            send_sem=rim_send.at[i], recv_sem=rim_recv.at[i], device_id=(gz, gy + dy), device_id_type=MESH)

    def e_face(dz, dy):
        i = 9 + (dz + 1) * 3 + dy + 1
        here, there = (pl.ds(1, 3), pl.ds(1, 3)) if dy == 0 else (pl.ds(2 + dy, 1), pl.ds(2 - 2 * dy, 1))
        return pltpu.make_async_remote_copy(
            src_ref=eext.at[2 + dz, here], dst_ref=eext.at[2 - 2 * dz, there],
            send_sem=rim_send.at[i], recv_sem=rim_recv.at[i], device_id=(gz + dz, gy + dy), device_id_type=MESH)

    def when_exists(dz, dy, make, act):
        @pl.when(exists(dz, dy))
        def _():
            getattr(make(), act)()

    def side_tiles(up, zu):
        z = (1 - up) * (2 - zu) + up * zu
        for k in range(zu + 1):
            corr_rows(z, (1 - up) * (2 - k) + up * (6 + k))
        return z

    for k in range(3):
        rows_recv(1, k)
    for zu in range(3):
        side_tiles(1 - odd, zu)
    collect(1)

    @pl.when(has_relay)
    def _():
        for k in range(3):
            rows_recv(2, k)

            @pl.when(at_cross)
            def _():
                far_relay(k).wait_recv()
    for zu in (2, 1, 0):
        z = side_tiles(odd, zu)
        encode(z)
        for dy in (-1, 1):
            when_exists(0, dy, lambda: e_rows(z, dy), "start")
        if zu != 1:
            dz = (zu - 1) * (2 * odd - 1)
            for dy in (0, -1, 1):
                when_exists(dz, dy, lambda: e_face(dz, dy), "start")

    def field(ref):
        cols = []
        for p in range(9):
            z, y = p // 3, p % 3
            cols.append(jnp.concatenate([ref[z + a, y + b] for a in range(3) for b in range(3)], axis=0))
        return jnp.concatenate(cols, axis=1)

    def shifted(parts, p):
        lane = iota((parts[0].shape[0], 128), 1)
        cut = slice(p * 128, (p + 1) * 128)
        left = jnp.where(lane == 0, 0.0, pltpu.roll(parts[0][:, cut], 1, 1))
        right = jnp.where(lane == 127, 0.0, pltpu.roll(parts[2][:, cut], 127, 1))
        return left + parts[1][:, cut] + right

    rim_recv_all(0, hext)
    ph[...] = jnp.dot(wh[0:576], field(hext), preferred_element_type=F32)
    for dy in (-1, 1):
        for z in range(3):
            when_exists(0, -dy, lambda: e_rows(z, dy), "wait_recv")
    for dz in (-1, 1):
        for dy in (-1, 0, 1):
            when_exists(-dz, -dy, lambda: e_face(dz, dy), "wait_recv")
    pe[0:288] = jnp.dot(we[0:288], field(eext), preferred_element_type=F32) + ph[0:288]

    def pick(ref, base):
        return [ref[base + c * 96:base + (c + 1) * 96] for c in range(3)]

    res_bias = column(b_res[...])
    for p in range(9):
        z, y = p // 3, p % 3
        r = jax.nn.sigmoid(shifted(pick(pe, 0), p) + res_bias)
        gext[1 + z, 1 + y] = (r * hext[1 + z, 1 + y].astype(F32)).astype(BF16)
    rim_start(2, gext)
    spread(2)
    collect(2)

    pe[288:864] = jnp.dot(we[288:864], field(eext), preferred_element_type=F32)
    for c in range(3):
        ph[288 + c * 96:288 + (c + 1) * 96] += pe[288 + c * 96:288 + (c + 1) * 96]
    upd_bias = column(b_upd[...])
    cand_bias = column(b_cand[...])
    for p in range(9):
        ph[0:96, p * 128:(p + 1) * 128] = jax.nn.sigmoid(shifted(pick(ph, 288), p) + upd_bias)
    rim_recv_all(2, gext)
    pe[0:288] = jnp.dot(wh[576:864], field(gext), preferred_element_type=F32) + pe[576:864]
    for p in range(9):
        z, y = p // 3, p % 3
        cand = jnp.tanh(shifted(pick(pe, 0), p) + cand_bias)
        u = ph[0:96, p * 128:(p + 1) * 128]
        new = ((1.0 - u) * hext[1 + z, 1 + y].astype(F32) + u * cand).astype(BF16)
        sext[:, p * 128:(p + 1) * 128] = new
        state_out[z, y] = new

    def head_copy(d):
        dz, dy = DIRS[d]
        here = [pl.ds(1, 3) if o == 0 else pl.ds(2 + 2 * o, 1) for o in (dz, dy)]
        there = [pl.ds(0, 3) if o == 0 else pl.ds(1 - o, 1) for o in (dz, dy)]
        return pltpu.make_async_remote_copy(
            src_ref=hsend.at[here[0], here[1]], dst_ref=hrecv.at[d, there[0], there[1]],
            send_sem=rim_send.at[27 + d], recv_sem=rim_recv.at[27 + d],
            device_id=(gz + dz, gy + dy), device_id_type=MESH)

    pe[0:216] = jnp.dot(whead[:, 0:96], sext[...], preferred_element_type=F32)
    for qz in (0, 4, 1, 2, 3):
        for qy in range(5):
            sums = [None] * 3
            for a in range(3):
                for b in range(3):
                    z, y = qz + a - 2, qy + b - 2
                    if 0 <= z < 3 and 0 <= y < 3:
                        for c in range(3):
                            row = ((a * 3 + b) * 3 + c) * 8
                            v = pe[row:row + 8, (z * 3 + y) * 128:(z * 3 + y + 1) * 128]
                            sums[c] = v if sums[c] is None else sums[c] + v
            left = jnp.where(lane8 == 0, 0.0, pltpu.roll(sums[0], 1, 1))
            right = jnp.where(lane8 == 127, 0.0, pltpu.roll(sums[2], 127, 1))
            hsend[qz, qy] = left + sums[1] + right
        if qz in (0, 4):
            for d, (dz, dy) in enumerate(DIRS):
                if dz == (qz - 2) // 2:
                    when_exists(dz, dy, lambda: head_copy(d), "start")

    for d, (dz, dy) in enumerate(DIRS):
        if dz == 0:
            when_exists(dz, dy, lambda: head_copy(d), "start")
    for d, (dz, dy) in enumerate(DIRS):
        when_exists(-dz, -dy, lambda: head_copy(d), "wait_recv")
    for p in range(9):
        z, y = p // 3, p % 3
        out = hsend[1 + z, 1 + y]
        for d, (dz, dy) in enumerate(DIRS):
            if (dz == 0 or z == 1 - dz) and (dy == 0 or y == 1 - dy):
                out = out + hrecv[d, z, y]
        for o in range(3):
            motion_out[z, y, o:o + 1] = motion[z, y, o:o + 1] + out[o:o + 1] + b_head[0:1, o:o + 1]

    for k in range(3):
        partner_copy(k).wait_send()

        @pl.when(has_relay_dst)
        def _():
            relay_copy(k).wait_send()
        rows_sent(0, k)
        rows_sent(1, k)

        @pl.when(has_relay)
        def _():
            rows_sent(2, k)

        @pl.when(at_cross)
        def _():
            far_partner(k).wait_send()

            @pl.when(has_relay_dst)
            def _():
                far_relay(k).wait_send()
    for rnd, ref in ((0, hext), (2, gext)):
        rim_sent(rnd, ref)
    for dy in (-1, 1):
        for z in range(3):
            when_exists(0, dy, lambda: e_rows(z, dy), "wait_send")
    for dz in (-1, 1):
        for dy in (-1, 0, 1):
            when_exists(dz, dy, lambda: e_face(dz, dy), "wait_send")
    for d, (dz, dy) in enumerate(DIRS):
        when_exists(dz, dy, lambda: head_copy(d), "wait_send")


def hand_on(a, b, c, d):
    c[...] = a[...]
    d[...] = b[...]


def solution(mesh):
    nz, ny = mesh.shape["gz"], mesh.shape["gy"]

    def on_device(source, target, hidden, motion, w_corr, w_motion, bias_encoder, w_update, bias_update, w_reset, bias_reset,
                  w_cand, bias_cand, w_head, bias_head):
        hbm = pl.BlockSpec(memory_space=pl.ANY)
        vmem = pl.BlockSpec(memory_space=pltpu.VMEM)
        ext = pltpu.VMEM((5, 5, 96, 128), BF16)
        made = pl.pallas_call(
            functools.partial(kernel, nz, ny),
            name="dvc_update",
            out_shape=(jax.ShapeDtypeStruct((3, 3, 96, 128), BF16), jax.ShapeDtypeStruct((3, 3, 3, 128), F32)),
            in_specs=[hbm, hbm, hbm, vmem, vmem, vmem, vmem, hbm, vmem, hbm, vmem, hbm, vmem, vmem, vmem],
            out_specs=(vmem, vmem),
            scratch_shapes=[
                pltpu.VMEM((3, 3, 128, 128), BF16),
                pltpu.VMEM((9, 9, 128, 128), BF16),
                ext, ext, ext,
                pltpu.VMEM((96, 1152), BF16),
                pltpu.VMEM((5, 5, 8, 128), F32), pltpu.VMEM((8, 3, 3, 8, 128), F32),
                pltpu.VMEM((3, 27, 18432), BF16),
                pltpu.VMEM((3072, 128), F32), pltpu.VMEM((3072, 128), F32),
                pltpu.VMEM((864, 864), BF16), pltpu.VMEM((864, 864), BF16),
                pltpu.VMEM((96, 896), BF16),
                pltpu.VMEM((216, 128), BF16), pltpu.VMEM((216, 128), F32),
                pltpu.VMEM((1152, 128), BF16),
                pltpu.VMEM((1152, 896), BF16),
                pltpu.VMEM((576, 1152), F32),
                pltpu.VMEM((864, 1152), F32),
                pltpu.SemaphoreType.DMA((6,)),
                pltpu.SemaphoreType.DMA((30,)), pltpu.SemaphoreType.DMA((30,)),
                pltpu.SemaphoreType.DMA((42,)), pltpu.SemaphoreType.DMA((42,)),
            ],
            compiler_params=pltpu.CompilerParams(
                collective_id=0, has_side_effects=True, vmem_limit_bytes=60 * 2 ** 20),
        )(source, target, hidden, motion, w_corr, w_motion.T, bias_encoder[None], w_update, bias_update[None], w_reset,
          bias_reset[None], w_cand, bias_cand[None], w_head.transpose(1, 0, 2), bias_head[None])
        return pl.pallas_call(
            hand_on, name="hand_on",
            out_shape=(jax.ShapeDtypeStruct((3, 3, 96, 128), BF16), jax.ShapeDtypeStruct((3, 3, 3, 128), F32)),
            in_specs=[vmem, vmem], out_specs=(vmem, vmem),
        )(*made)

    rows = P("gz", "gy", None, None)
    return jax.shard_map(
        on_device, mesh=mesh, in_specs=(rows,) * 4 + (P(),) * 11, out_specs=(rows, rows), check_vma=False)
```
